256 devices in a mesh: ep: 64 (over y, z, core), tp: 4 (over x).
Axes of the slice: x: 4, y: 4, z: 8, core: 2. Of those that a mesh axis runs over, the one named last changes fastest.
Arguments:
- tokens: bfloat16 [2048, 4096], P('ep'), may hold values from -6 to 6
- expert_ids: int32 [2048, 8], P('ep'), may hold values from 0 to 63, all different within a row; in each aligned block of 32 rows (0 to 31, 32 to 63, ...) at most 4 rows name the same one
- gates: float32 [2048, 8], P('ep'), may hold values from 0.05 to 0.5
- w_gate: bfloat16 [64, 768, 4096], P('ep', 'tp'), may hold values from -0.09375 to 0.09375
- w_up: bfloat16 [64, 768, 4096], P('ep', 'tp'), may hold values from -0.09375 to 0.09375
- w_down: bfloat16 [64, 768, 4096], P('ep', 'tp'), may hold values from -0.21875 to 0.21875
- grad_out: bfloat16 [2048, 4096], P('ep'), may hold values from -6 to 6
Outputs:
- layer_out: bfloat16 [2048, 4096], P('ep')
- gate_grads: float32 [2048, 8], P('ep')
- token_grads: bfloat16 [2048, 4096], P('ep')
- grad_gate: bfloat16 [64, 768, 4096], P('ep', 'tp')
- grad_up: bfloat16 [64, 768, 4096], P('ep', 'tp')
- grad_down: bfloat16 [64, 768, 4096], P('ep', 'tp')
The draws below stay inside these ranges and needn't reach their ends.
Inputs may be any that keep to these rules, and one draw needn't show every extreme that they name: `expert_ids`: each row names 8 different experts. Among the rows of one device no expert is named by more than 4 rows, and in some device's rows an expert is named by exactly 4.
All inputs are finite; a program needn't handle non-finite values.
Results may differ from the reference program's by a relative error of at most 0.012.
Values may be sent and summed in bfloat16 or wider, within the bound.
No kernel may reach another device: no remote copies, remote signals or barrier semaphores. Data moves between devices by JAX's collectives and lax.ppermute only.
A program may use at most 128 MiB of HBM per device.

```python
import math
import jax
import jax.numpy as jnp
import numpy as np
from jax import lax

D = 4096
TOP = 8
FF = 768
TOK_DEV = 32
EXPERTS = 64
CAP = 4
TOKENS = 2048
N_EP = 64
N_TP = 4


def block_scale(rng, dims, shards, least, high):
    def one(position, blocks):
        steps = jax.random.uniform(jax.random.fold_in(jax.random.fold_in(rng, 6), position), (blocks,), jnp.float32, least / len(shards), high / len(shards))
        return jnp.repeat(jnp.exp(steps), dims[position] // blocks).reshape((-1,) + (1,) * (len(dims) - position - 1))

    factor_of = one(*shards[0])
    for cut in shards[1:]:
        factor_of = factor_of * one(*cut)
    return factor_of


def assign_block(own_key, own, number, rows, number_of, top, limit, slope):
    sequence = jax.random.permutation(own_key, number_of)
    packed, ordinary = shares(number_of, rows * top, limit, slope, True), shares(number_of, rows * top, limit, slope, False)
    places = jnp.arange(number_of)

    def named(sizes, offset_by):
        used = int((sizes > 0).sum())
        fixed = max(1, used // 4)
        shifted = fixed + (places - fixed + offset_by * (used - fixed)) % max(1, number_of - fixed)
        return jnp.zeros((number_of,), jnp.int32).at[sequence[jnp.where(places < fixed, places, shifted)]].set(jnp.asarray(sizes, jnp.int32))

    sizes = jnp.where(number % 4 == 0, named(packed, number // 4), named(ordinary, number - number // 4 - 1))
    mixed = jax.random.permutation(jax.random.fold_in(own, 3), number_of)
    donor, receiver = mixed[0:number_of // 2 * 2:2], mixed[1:number_of // 2 * 2:2]
    slack = jnp.minimum(sizes[donor] - 1, limit - sizes[receiver]) // 2
    slack = jnp.where((donor == sequence[0]) | (receiver == sequence[0]) | (sizes[receiver] == 0), 0, jnp.maximum(slack, 0))
    shifted = jax.random.randint(jax.random.fold_in(own, 4), (number_of // 2,), 0, 1 << 20) % (slack + 1)
    sizes = sizes.at[donor].add(-shifted).at[receiver].add(shifted)
    labels = jnp.searchsorted(jnp.cumsum(sizes), jnp.arange(rows * top), side="right").astype(jnp.int32)
    listing = labels.reshape(top, rows).T
    listing = listing[jax.random.permutation(jax.random.fold_in(own, 1), rows)]
    offset_by = jax.random.randint(jax.random.fold_in(own, 2), (rows, 1), 0, top)
    return jnp.take_along_axis(listing, (jnp.arange(top)[None, :] + offset_by) % top, axis=1)


def shares(count, total, bound, skew, full):
    weights = [(1 << 20) // math.isqrt(standing ** skew) + 1 for standing in range(1, count + 1)]
    largest = bound if full else min(bound, max(-(-total // count), total * weights[0] // sum(weights)))
    least = 1 if total - largest >= count - 1 else 0
    given, spare = [largest] + [least] * (count - 1), total - largest - least * (count - 1)
    while spare > 0:
        movable = [i for i in range(1, count) if given[i] < largest] or [i for i in range(1, count) if given[i] < bound]
        pool, budget = sum([weights[i] for i in movable]), spare
        for i in movable:
            more = min(bound - given[i], max(1, budget * weights[i] // pool), spare)
            given[i] = given[i] + more
            spare = spare - more
    return np.array(given)


def scatter_about(stream_key, extent, deviation, most, cuts=(), held_as=jnp.bfloat16):
    gain = block_scale(stream_key, extent, cuts, -0.22, 0.18) if cuts else 1.0
    values = jax.random.normal(stream_key, extent, jnp.float32) * deviation * gain
    return jnp.minimum(jnp.maximum(values, -most), most).astype(held_as)


def setup_inputs(seed: int = 0) -> dict:
    keys = jax.random.split(jax.random.key(seed), 8)
    tokens = scatter_about(keys[0], (TOKENS, D), 1.0, 6.0, ((0, 64),))
    expert_ids_keys = jax.random.split(jax.random.fold_in(keys[1], 1), TOKENS // TOK_DEV)
    expert_ids_turns = jax.random.permutation(jax.random.fold_in(keys[1], 3), TOKENS // TOK_DEV)
    expert_ids = jax.vmap(lambda own, number: assign_block(jax.random.fold_in(keys[1], 2), own, number, TOK_DEV, EXPERTS, TOP, CAP, 2))(expert_ids_keys, expert_ids_turns).reshape((TOKENS, TOP))
    gates = jnp.clip(jnp.exp(math.log(0.5) - 2.3025851 * jax.random.uniform(keys[2], (TOKENS, TOP), jnp.float32) ** block_scale(keys[2], (TOKENS, TOP), ((0, 64),), -0.2, 0.2)), 0.05, 0.5)
    w_gate = scatter_about(keys[3], (EXPERTS, FF, D), D ** -0.5, 0.09375, ((0, 64), (1, 4)))
    w_up = scatter_about(keys[4], (EXPERTS, FF, D), D ** -0.5, 0.09375, ((0, 64), (1, 4)))
    w_down = scatter_about(keys[5], (EXPERTS, FF, D), FF ** -0.5, 0.21875, ((0, 64), (1, 4)))
    grad_out = scatter_about(keys[6], (TOKENS, D), 1.0, 6.0, ((0, 64),))
    return {"tokens": tokens, "expert_ids": expert_ids, "gates": gates, "w_gate": w_gate, "w_up": w_up, "w_down": w_down, "grad_out": grad_out}


def reference(tokens, expert_ids, gates, w_gate, w_up, w_down, grad_out):
    pairs = TOK_DEV * TOP
    chosen_ids = expert_ids.reshape(N_EP, pairs)
    onehot = (chosen_ids[:, :, None] == jnp.arange(EXPERTS, dtype=jnp.int32)[None, None, :]).astype(jnp.int32)
    before = jnp.cumsum(onehot, axis=1) - onehot
    slot_index = jnp.sum(before * onehot, axis=2).astype(jnp.int32)
    source_dev = jnp.broadcast_to(jnp.arange(N_EP, dtype=jnp.int32)[:, None], (N_EP, pairs))
    token_index = source_dev * TOK_DEV + (jnp.arange(pairs, dtype=jnp.int32) // TOP)[None, :]
    sources = jnp.full((EXPERTS, CAP, N_EP), TOKENS, dtype=jnp.int32)
    sources = sources.at[chosen_ids, slot_index, source_dev].set(token_index.astype(jnp.int32))
    gate_table = jnp.zeros((EXPERTS, CAP, N_EP), jnp.float32)
    gate_table = gate_table.at[chosen_ids, slot_index, source_dev].set(gates.reshape(N_EP, pairs))
    token_pad = jnp.concatenate([tokens, jnp.zeros((1, D), tokens.dtype)], axis=0)
    grad_pad = jnp.concatenate([grad_out, jnp.zeros((1, D), grad_out.dtype)], axis=0)
    row_count = CAP * N_EP
    quarter_width = FF // N_TP

    def quarter_sum(left_mat, right_mat):
        left_q = left_mat.astype(jnp.float32).reshape(row_count, N_TP, quarter_width)
        right_q = right_mat.astype(jnp.float32).reshape(N_TP, quarter_width, D)
        return jnp.einsum("rqf,qfd->qrd", left_q, right_q, precision=lax.Precision.HIGHEST)

    def expert_work(expert):
        rows_from = sources[expert]
        x_rows = token_pad[rows_from].reshape(row_count, D)
        g_rows = (gate_table[expert][:, :, None] * grad_pad[rows_from].astype(jnp.float32)).astype(jnp.bfloat16).reshape(row_count, D)
        gate_mat = w_gate[expert]
        up_mat = w_up[expert]
        down_mat = w_down[expert]
        pre_gate = jnp.dot(x_rows, gate_mat.T, preferred_element_type=jnp.float32)
        pre_up = jnp.dot(x_rows, up_mat.T, preferred_element_type=jnp.float32)
        sigmoid_gate = jax.nn.sigmoid(pre_gate)
        activated = pre_gate * sigmoid_gate
        hidden = (activated * pre_up).astype(jnp.bfloat16)
        parts = lax.optimization_barrier(quarter_sum(hidden, down_mat).astype(jnp.bfloat16))
        out_rows = jnp.sum(parts.astype(jnp.float32), axis=0).astype(jnp.bfloat16)
        grad_hidden = jnp.dot(g_rows, down_mat.T, preferred_element_type=jnp.float32)
        d_up = (grad_hidden * activated).astype(jnp.bfloat16)
        d_gate = (grad_hidden * pre_up * sigmoid_gate * (1.0 + pre_gate * (1.0 - sigmoid_gate))).astype(jnp.bfloat16)
        grad_down_e = jnp.dot(hidden.T, g_rows, preferred_element_type=jnp.float32).astype(jnp.bfloat16)
        grad_gate_e = jnp.dot(d_gate.T, x_rows, preferred_element_type=jnp.float32).astype(jnp.bfloat16)
        grad_up_e = jnp.dot(d_up.T, x_rows, preferred_element_type=jnp.float32).astype(jnp.bfloat16)
        back_parts = quarter_sum(d_gate, gate_mat) + quarter_sum(d_up, up_mat)
        back_parts = lax.optimization_barrier(back_parts.astype(jnp.bfloat16))
        back_rows = jnp.sum(back_parts.astype(jnp.float32), axis=0).astype(jnp.bfloat16)
        return (out_rows.reshape(CAP, N_EP, D), back_rows.reshape(CAP, N_EP, D), grad_gate_e, grad_up_e, grad_down_e)

    out_all, back_all, grad_gate, grad_up, grad_down = lax.map(expert_work, jnp.arange(EXPERTS, dtype=jnp.int32))
    picked_out = out_all[chosen_ids, slot_index, source_dev].reshape(TOKENS, TOP, D).astype(jnp.float32)
    picked_back = back_all[chosen_ids, slot_index, source_dev].reshape(TOKENS, TOP, D).astype(jnp.float32)
    layer_out = jnp.einsum("tk,tkd->td", gates, picked_out, precision=lax.Precision.HIGHEST).astype(jnp.bfloat16)
    gate_grads = jnp.einsum("tkd,td->tk", picked_out, grad_out.astype(jnp.float32), precision=lax.Precision.HIGHEST)
    token_grads = jnp.sum(picked_back, axis=1).astype(jnp.bfloat16)
    return (layer_out, gate_grads, token_grads, grad_gate, grad_up, grad_down)
```

```python
import functools

import jax
import jax.numpy as jnp
from jax import lax
from jax.experimental import pallas as pl
from jax.experimental.pallas import tpu as pltpu
from jax.sharding import PartitionSpec as P

HALF = 4
BLOCK = 2 * HALF
NT = (((1,), (1,)), ((), ()))
TN = (((0,), (0,)), ((), ()))


def row_facts(shape, dim):
    row = lax.broadcasted_iota(jnp.int32, shape, dim)
    slot = lax.rem(row, HALF).astype(jnp.float32)
    second = lax.rem(lax.div(row, HALF), 2) == 1
    return lax.div(row, BLOCK), slot, second


def dot(left, right, dims=(((1,), (0,)), ((), ()))):
    return lax.dot_general(left, right, dims, preferred_element_type=jnp.float32)


def dispatch_kernel(quarter, ids_ref, gates_ref, tok_ref, dy_ref, out_ref):
    chosen, count = ids_ref.shape
    shape = (out_ref.shape[0], count)
    expert, slot, second = row_facts(shape, 0)
    named = jnp.zeros(shape, jnp.float32)
    gate = jnp.zeros(shape, jnp.float32)
    for k in range(chosen):
        hit = ids_ref[k : k + 1, :] == expert
        named = named + jnp.where(hit, 1.0, 0.0)
        gate = gate + jnp.where(hit, gates_ref[k : k + 1, :], 0.0)
    earlier = lax.broadcasted_iota(jnp.int32, (count, count), 0) < lax.broadcasted_iota(
        jnp.int32, (count, count), 1
    )
    before = dot(named.astype(jnp.bfloat16), jnp.where(earlier, 1.0, 0.0).astype(jnp.bfloat16))
    pick = jnp.where(before == slot, named, 0.0)
    scale = jnp.sum(pick * jnp.where(second, gate, 1.0), axis=1, keepdims=True)
    pick_x = jnp.where(second, 0.0, pick).astype(jnp.bfloat16)
    pick_g = jnp.where(second, pick, 0.0).astype(jnp.bfloat16)
    rows = dot(pick_x, tok_ref[...]) + dot(pick_g, dy_ref[...])
    out_ref[...] = (scale * rows).astype(jnp.bfloat16)


def expert_kernel(quarters, x_ref, wg_ref, wu_ref, wd_ref, out_ref, act_ref, pre, back):
    step = pl.program_id(0)

    @pl.when(step == 0)
    def _():
        rows = x_ref[0]
        for j, w_ref in enumerate((wg_ref, wu_ref, wd_ref)):
            pre[j] = dot(rows, w_ref[...], NT)

    @pl.when(jnp.logical_and(step > 0, step < quarters))
    def _():
        rows = x_ref[0]
        for j, w_ref in enumerate((wg_ref, wu_ref, wd_ref)):
            pre[j] += dot(rows, w_ref[...], NT)

    @pl.when(step == quarters)
    def _():
        a, b = pre[0], pre[1]
        row_count = a.shape[0]
        dh = pltpu.roll(pre[2], row_count - HALF, 0)
        second = row_facts(a.shape, 0)[2]
        sig = jax.nn.sigmoid(a)
        act = a * sig
        hidden = jnp.where(second, 0.0, act * b)
        d_up = jnp.where(second, 0.0, dh * act)
        d_gate = jnp.where(second, 0.0, dh * b * sig * (1.0 + a * (1.0 - sig)))
        back[0] = hidden.astype(jnp.bfloat16)
        back[1] = pltpu.roll(d_gate, HALF, 0).astype(jnp.bfloat16)
        back[2] = pltpu.roll(d_up, HALF, 0).astype(jnp.bfloat16)
        act_ref[0] = d_gate.astype(jnp.bfloat16)
        act_ref[1] = d_up.astype(jnp.bfloat16)
        act_ref[2] = pltpu.roll(hidden, HALF, 0).astype(jnp.bfloat16)

    @pl.when(step >= quarters)
    def _():
        total = dot(back[0], wd_ref[...]) + dot(back[1], wg_ref[...]) + dot(back[2], wu_ref[...])
        out_ref[0] = total.astype(jnp.bfloat16)


def weight_kernel(act_ref, x_ref, gg_ref, gu_ref, gd_ref):
    rows = x_ref[0]
    for j, out_ref in enumerate((gg_ref, gu_ref, gd_ref)):
        out_ref[...] = dot(act_ref[j], rows, TN).astype(jnp.bfloat16)


def combine_kernel(quarter, ids_ref, gates_ref, dy_ref, rows_ref, out_ref):
    count, chosen = ids_ref.shape
    width = dy_ref.shape[1]
    rows = rows_ref[...]
    shape = (count, rows.shape[0])
    expert, slot, second = row_facts(shape, 1)
    hits = [ids_ref[:, k : k + 1] == expert for k in range(chosen)]
    named = jnp.zeros(shape, jnp.float32)
    gate = jnp.zeros(shape, jnp.float32)
    for k in range(chosen):
        named = named + jnp.where(hits[k], 1.0, 0.0)
        gate = gate + jnp.where(hits[k], gates_ref[:, k : k + 1], 0.0)
    earlier = lax.broadcasted_iota(jnp.int32, (count, count), 1) < lax.broadcasted_iota(
        jnp.int32, (count, count), 0
    )
    before = dot(jnp.where(earlier, 1.0, 0.0).astype(jnp.bfloat16), named.astype(jnp.bfloat16))
    pick = jnp.where(before == slot, named, 0.0)
    pick_y = jnp.where(second, 0.0, pick)
    pick_r = jnp.where(second, pick, 0.0).astype(jnp.bfloat16)
    weight = pick_y * gate
    high = weight.astype(jnp.bfloat16)
    low = (weight - high.astype(jnp.float32)).astype(jnp.bfloat16)
    out_ref[0:count, 0:width] = (dot(high, rows) + dot(low, rows)).astype(jnp.bfloat16)
    out_ref[count : 2 * count, 0:width] = dot(pick_r, rows).astype(jnp.bfloat16)
    products = pick_y * dot(dy_ref[...], rows, NT)
    lane = lax.broadcasted_iota(jnp.int32, (count, 128), 1)
    share = jnp.zeros((count, 128), jnp.float32)
    for k in range(chosen):
        value = jnp.sum(jnp.where(hits[k], products, 0.0), axis=1, keepdims=True)
        share = share + jnp.where(lax.rem(lane, chosen) == k, value, 0.0)
    first = share.astype(jnp.bfloat16).astype(jnp.float32)
    rest = share - first
    middle = rest.astype(jnp.bfloat16).astype(jnp.float32)
    parts = jnp.where(lane < chosen, first, jnp.where(lane < 2 * chosen, middle, rest - middle))
    out_ref[0:count, width : width + 128] = parts.astype(jnp.bfloat16)
    out_ref[count : 2 * count, width : width + 128] = jnp.zeros((count, 128), jnp.bfloat16)


def finish_kernel(parts_ref, layer_ref, gate_ref, token_ref):
    quarters = parts_ref.shape[0]
    count, chosen = gate_ref.shape
    width = layer_ref.shape[1] // quarters
    share = jnp.zeros((count, 128), jnp.float32)
    for q in range(quarters):
        span = slice(q * width, (q + 1) * width)
        layer_ref[:, span] = parts_ref[q, 0:count, 0:width]
        token_ref[:, span] = parts_ref[q, count : 2 * count, 0:width]
        share = share + parts_ref[q, 0:count, width : width + 128].astype(jnp.float32)
    total = share[:, 0:chosen]
    for j in range(1, 3):
        total = total + share[:, j * chosen : (j + 1) * chosen]
    gate_ref[...] = total


def spec(shape, index):
    return pl.BlockSpec(shape, index)


def on_device(tokens, expert_ids, gates, w_gate, w_up, w_down, grad_out):
    count, model_width = tokens.shape
    chosen = expert_ids.shape[1]
    hidden = w_gate.shape[1]
    experts = lax.axis_size("ep")
    quarters = lax.axis_size("tp")
    width = model_width // quarters
    rows = experts * BLOCK
    quarter = lax.axis_index("tp").astype(jnp.int32).reshape(1)
    bf16 = jnp.bfloat16
    params = pltpu.CompilerParams(vmem_limit_bytes=40 * 1024 * 1024)

    whole = lambda i, q: (0, 0)
    mine = lambda i, q: (0, q[0])
    sent = pl.pallas_call(
        dispatch_kernel,
        name="dispatch",
        grid_spec=pltpu.PrefetchScalarGridSpec(
            num_scalar_prefetch=1,
            grid=(1,),
            in_specs=[
                spec((chosen, count), whole),
                spec((chosen, count), whole),
                spec((count, width), mine),
                spec((count, width), mine),
            ],
            out_specs=spec((rows, width), whole),
        ),
        out_shape=jax.ShapeDtypeStruct((rows, width), bf16),
        compiler_params=params,
    )(quarter, expert_ids.T, gates.T, tokens, grad_out)

    block = (experts, BLOCK, width)
    arrived = lax.all_to_all(sent.reshape(block), "ep", 0, 0, tiled=True).reshape(rows, width)
    gathered = lax.all_to_all(
        jnp.broadcast_to(arrived[None], (quarters, rows, width)), "tp", 0, 0, tiled=True
    )

    weight_spec = spec((None, hidden, width), lambda i: (0, 0, lax.rem(i, quarters)))
    partial, acts = pl.pallas_call(
        functools.partial(expert_kernel, quarters),
        name="expert",
        grid=(2 * quarters,),
        in_specs=[spec((1, rows, width), lambda i: (jnp.minimum(i, quarters - 1), 0, 0))]
        + [weight_spec] * 3,
        out_specs=(
            spec((1, rows, width), lambda i: (jnp.maximum(i - quarters, 0), 0, 0)),
            spec((3, rows, hidden), lambda i: (0, 0, 0)),
        ),
        out_shape=(
            jax.ShapeDtypeStruct((quarters, rows, width), bf16),
            jax.ShapeDtypeStruct((3, rows, hidden), bf16),
        ),
        scratch_shapes=[
            pltpu.VMEM((3, rows, hidden), jnp.float32),
            pltpu.VMEM((3, rows, hidden), bf16),
        ],
        compiler_params=params,
    )(gathered, w_gate, w_up, w_down)

    shares = lax.all_to_all(partial, "tp", 0, 0, tiled=True)
    summed = jnp.sum(shares.astype(jnp.float32), axis=0).astype(bf16)
    returned = lax.all_to_all(summed.reshape(block), "ep", 0, 0, tiled=True).reshape(rows, width)

    grad_shape = jax.ShapeDtypeStruct(w_gate.shape, bf16)
    grad_gate, grad_up, grad_down = pl.pallas_call(
        weight_kernel,
        name="weights",
        grid=(quarters,),
        in_specs=[
            spec((3, rows, hidden), lambda i: (0, 0, 0)),
            spec((1, rows, width), lambda i: (i, 0, 0)),
        ],
        out_specs=(spec((None, hidden, width), lambda i: (0, 0, i)),) * 3,
        out_shape=(grad_shape,) * 3,
        compiler_params=params,
        cost_estimate=pl.CostEstimate(
            flops=6 * rows * hidden * model_width,
            bytes_accessed=2 * model_width * (rows + 3 * hidden),
            transcendentals=0,
        ),
    )(acts, gathered)

    packed = pl.pallas_call(
        combine_kernel,
        name="combine",
        grid_spec=pltpu.PrefetchScalarGridSpec(
            num_scalar_prefetch=1,
            grid=(1,),
            in_specs=[
                spec((count, chosen), whole),
                spec((count, chosen), whole),
                spec((count, width), mine),
                spec((rows, width), whole),
            ],
            out_specs=spec((2 * count, width + 128), whole),
        ),
        out_shape=jax.ShapeDtypeStruct((2 * count, width + 128), bf16),
        compiler_params=params,
    )(quarter, expert_ids, gates, grad_out, returned)
    pieces = lax.all_to_all(
        jnp.broadcast_to(packed[None], (quarters,) + packed.shape), "tp", 0, 0, tiled=True
    )
    layer_out, gate_grads, token_grads = pl.pallas_call(
        finish_kernel,
        name="finish",
        out_shape=(
            jax.ShapeDtypeStruct((count, model_width), bf16),
            jax.ShapeDtypeStruct((count, chosen), jnp.float32),
            jax.ShapeDtypeStruct((count, model_width), bf16),
        ),
        compiler_params=params,
    )(pieces)
    return layer_out, gate_grads, token_grads, grad_gate, grad_up, grad_down


def solution(mesh):
    rows, cut = P("ep", None), P("ep", "tp", None)
    return jax.shard_map(
        on_device,
        mesh=mesh,
        in_specs=(rows, rows, rows, cut, cut, cut, rows),
        out_specs=(rows, rows, rows, cut, cut, cut),
        check_vma=False,
    )
```

```python
import jax
import jax.numpy as jnp
from jax import lax
from jax.experimental import pallas as pl
from jax.experimental.pallas import tpu as pltpu
from jax.sharding import PartitionSpec as P

SLOTS = 4
NN = (((1,), (0,)), ((), ()))
NT = (((1,), (1,)), ((), ()))
TN = (((0,), (0,)), ((), ()))
F32 = jnp.float32
BF16 = jnp.bfloat16
VMEM = pl.BlockSpec(memory_space=pltpu.VMEM)
SMEM = pl.BlockSpec(memory_space=pltpu.SMEM)
PARAMS = pltpu.CompilerParams(vmem_limit_bytes=12 * 1024 * 1024)


def dot(left, right, dims=NN):
    return lax.dot_general(left, right, dims, preferred_element_type=F32)


def cost(flops, moved):
    return pl.CostEstimate(flops=flops, bytes_accessed=moved, transcendentals=0)


def at_quarter(ref, quarter, width):
    return ref[0, :, pl.ds(pl.multiple_of(quarter * width, width), width)]


def row_facts(shape, dim):
    row = lax.broadcasted_iota(jnp.int32, shape, dim)
    return lax.div(row, SLOTS), lax.rem(row, SLOTS).astype(F32)


def picks_by_token(ids_ref, gates_ref, row_count):
    count, chosen = ids_ref.shape
    shape = (count, row_count)
    expert, slot = row_facts(shape, 1)
    hits = [ids_ref[:, k : k + 1] == expert for k in range(chosen)]
    named = jnp.zeros(shape, F32)
    gate = jnp.zeros(shape, F32)
    for k in range(chosen):
        named = named + jnp.where(hits[k], 1.0, 0.0)
        gate = gate + jnp.where(hits[k], gates_ref[:, k : k + 1], 0.0)
    rows = lax.broadcasted_iota(jnp.int32, (count, count), 0)
    earlier = jnp.where(lax.broadcasted_iota(jnp.int32, (count, count), 1) < rows, 1.0, 0.0)
    before = dot(earlier.astype(BF16), named.astype(BF16))
    return jnp.where(before == slot, named, 0.0), gate, hits


def dispatch_kernel(quarter, ids_ref, gates_ref, tok_ref, dy_ref, dy_next_ref, x_ref, g_ref):
    chosen, count = ids_ref.shape
    width = tok_ref.shape[1]
    shape = (x_ref.shape[0], count)
    expert, slot = row_facts(shape, 0)
    named = jnp.zeros(shape, F32)
    gate = jnp.zeros(shape, F32)
    for k in range(chosen):
        hit = ids_ref[k : k + 1, :] == expert
        named = named + jnp.where(hit, 1.0, 0.0)
        gate = gate + jnp.where(hit, gates_ref[k : k + 1, :], 0.0)
    cols = lax.broadcasted_iota(jnp.int32, (count, count), 1)
    earlier = jnp.where(lax.broadcasted_iota(jnp.int32, (count, count), 0) < cols, 1.0, 0.0)
    before = dot(named.astype(BF16), earlier.astype(BF16))
    pick = jnp.where(before == slot, named, 0.0)
    scale = jnp.sum(pick * gate, axis=1, keepdims=True)
    pick = pick.astype(BF16)
    x_ref[...] = dot(pick, tok_ref[...]).astype(BF16)
    g_ref[:, 0:width] = (scale * dot(pick, dy_ref[...])).astype(BF16)
    g_ref[:, width : 2 * width] = (scale * dot(pick, dy_next_ref[...])).astype(BF16)


def forward_kernel(q_ref, *refs):
    pieces, (wg_ref, wu_ref, wd_ref), outs = refs[:8], refs[8:11], refs[11:]
    partials, (hidden_ref, act_ref, slope_ref) = outs[:8], outs[8:]
    half, width = pieces[0].shape
    for part in range(2):
        a, b = None, None
        for j, ahead in enumerate((0, 3, 1, 2)):
            rows = pieces[2 * j + part][...]
            where = lax.rem(q_ref[0] + ahead, 4)
            a_new = dot(rows, at_quarter(wg_ref, where, width), NT)
            b_new = dot(rows, at_quarter(wu_ref, where, width), NT)
            a, b = (a_new, b_new) if a is None else (a + a_new, b + b_new)
        sig = jax.nn.sigmoid(a)
        act = a * sig
        hidden = (act * b).astype(BF16)
        span = slice(part * half, (part + 1) * half)
        hidden_ref[span, :] = hidden
        act_ref[span, :] = act
        slope_ref[span, :] = b * sig * (1.0 + a * (1.0 - sig))
        for j, ahead in enumerate((2, 1, 3, 0)):
            where = lax.rem(q_ref[0] + ahead, 4)
            partials[2 * j + part][...] = dot(hidden, at_quarter(wd_ref, where, width)).astype(BF16)


def backward_kernel(q_ref, *refs):
    pieces, (wg_ref, wu_ref, wd_ref, act_ref, slope_ref), outs = refs[:8], refs[8:13], refs[13:]
    partials, (gate_ref, up_ref) = outs[:8], outs[8:]
    half, width = pieces[0].shape
    for part in range(2):
        dh = None
        for j, ahead in enumerate((0, 1, 3, 2)):
            where = lax.rem(q_ref[0] + ahead, 4)
            new = dot(pieces[2 * j + part][...], at_quarter(wd_ref, where, width), NT)
            dh = new if dh is None else dh + new
        span = slice(part * half, (part + 1) * half)
        d_up = (dh * act_ref[span, :]).astype(BF16)
        d_gate = (dh * slope_ref[span, :]).astype(BF16)
        gate_ref[span, :] = d_gate
        up_ref[span, :] = d_up
        for j, ahead in enumerate((2, 1, 3, 0)):
            where = lax.rem(q_ref[0] + ahead, 4)
            total = dot(d_gate, at_quarter(wg_ref, where, width)) + dot(d_up, at_quarter(wu_ref, where, width))
            partials[2 * j + part][...] = total.astype(BF16)


def weight_kernel(order, q_ref, *refs):
    pieces, rest = refs[:8], refs[8:]
    acts, outs = rest[: len(rest) // 2], rest[len(rest) // 2 :]
    half, width = pieces[0].shape
    for act_ref, out_ref in zip(acts, outs):
        top, bottom = act_ref[0:half, :], act_ref[half : 2 * half, :]
        for j, ahead in enumerate(order):
            where = lax.rem(q_ref[0] + ahead, 4)
            total = dot(top, pieces[2 * j][...], TN) + dot(bottom, pieces[2 * j + 1][...], TN)
            out_ref[0, :, pl.ds(pl.multiple_of(where * width, width), width)] = total.astype(BF16)


def combine_out_kernel(quarter, ids_ref, gates_ref, dy_ref, rows_ref, out_ref):
    count, chosen = ids_ref.shape
    width = dy_ref.shape[1]
    rows = rows_ref[...]
    pick, gate, hits = picks_by_token(ids_ref, gates_ref, rows.shape[0])
    weight = pick * gate
    high = weight.astype(BF16)
    low = (weight - high.astype(F32)).astype(BF16)
    out_ref[:, 0:width] = (dot(high, rows) + dot(low, rows)).astype(BF16)
    products = pick * dot(dy_ref[...], rows, NT)
    lane = lax.broadcasted_iota(jnp.int32, (count, 128), 1)
    share = jnp.zeros((count, 128), F32)
    for k in range(chosen):
        value = jnp.sum(jnp.where(hits[k], products, 0.0), axis=1, keepdims=True)
        share = share + jnp.where(lax.rem(lane, chosen) == k, value, 0.0)
    first = share.astype(BF16).astype(F32)
    rest = share - first
    middle = rest.astype(BF16).astype(F32)
    parts = jnp.where(lane < chosen, first, jnp.where(lane < 2 * chosen, middle, rest - middle))
    out_ref[:, width : width + 128] = parts.astype(BF16)


def combine_back_kernel(ids_ref, gates_ref, rows_ref, out_ref):
    rows = rows_ref[...]
    pick = picks_by_token(ids_ref, gates_ref, rows.shape[0])[0]
    out_ref[...] = dot(pick.astype(BF16), rows).astype(BF16)


def finish_kernel(q_ref, *refs):
    outs, backs, (layer_ref, gate_ref, token_ref) = refs[:4], refs[4:8], refs[8:]
    count, chosen = gate_ref.shape
    width = backs[0].shape[1]
    share = jnp.zeros((count, 128), F32)
    for j, ahead in enumerate((0, 3, 1, 2)):
        span = pl.ds(pl.multiple_of(lax.rem(q_ref[0] + ahead, 4) * width, width), width)
        layer_ref[:, span] = outs[j][:, 0:width]
        token_ref[:, span] = backs[j][...]
        share = share + outs[j][:, width : width + 128].astype(F32)
    total = share[:, 0:chosen]
    for j in range(1, 3):
        total = total + share[:, j * chosen : (j + 1) * chosen]
    gate_ref[...] = total


def moved(value, ahead):
    return lax.ppermute(value, "tp", [(i, (i + ahead) % 4) for i in range(4)])


def gathered(top, bottom):
    left_t, right_b = moved(top, 1), moved(bottom, 3)
    left_b, right_t = moved(bottom, 1), moved(top, 3)
    far_t, far_b = moved(left_t, 1), moved(right_b, 3)
    return top, bottom, left_t, left_b, right_t, right_b, far_t, far_b


def total(*values):
    result = values[0].astype(F32)
    for value in values[1:]:
        result = result + value.astype(F32)
    return result.astype(BF16)


def scattered(partials):
    far_t, far_b, right_t, right_b, left_t, left_b, own_t, own_b = partials
    in_t, in_b = moved(far_t, 1), moved(far_b, 3)
    from_left_b, from_right_t = moved(right_b, 1), moved(left_t, 3)
    from_left_t = moved(total(right_t, in_t), 1)
    from_right_b = moved(total(left_b, in_b), 3)
    return total(own_t, from_left_t, from_right_t), total(own_b, from_left_b, from_right_b)


def swapped(rows, experts):
    block = rows.reshape(experts, SLOTS, rows.shape[-1])
    return lax.all_to_all(block, "ep", 0, 0, tiled=True)


def on_device(tokens, expert_ids, gates, w_gate, w_up, w_down, grad_out):
    count, model_width = tokens.shape
    chosen = expert_ids.shape[1]
    hidden = w_gate.shape[1]
    experts = lax.axis_size("ep")
    width = model_width // 4
    rows = experts * SLOTS
    half = rows // 2
    quarter = lax.axis_index("tp").astype(jnp.int32).reshape(1)
    shape = jax.ShapeDtypeStruct

    whole = lambda i, q: (0, 0)
    mine = lambda i, q: (0, q[0])
    ids_t, gates_t = expert_ids.T, gates.T
    sent_x, sent_g = pl.pallas_call(
        dispatch_kernel,
        name="dispatch",
        grid_spec=pltpu.PrefetchScalarGridSpec(
            num_scalar_prefetch=1,
            grid=(1,),
            in_specs=[
                pl.BlockSpec((chosen, count), whole),
                pl.BlockSpec((chosen, count), whole),
                pl.BlockSpec((count, width), mine),
                pl.BlockSpec((count, width), mine),
                pl.BlockSpec((count, width), lambda i, q: (0, lax.rem(q[0] + 1, 4))),
            ],
            out_specs=(pl.BlockSpec((rows, width), whole), pl.BlockSpec((rows, 2 * width), whole)),
        ),
        out_shape=(shape((rows, width), BF16), shape((rows, 2 * width), BF16)),
        compiler_params=PARAMS,
    )(quarter, ids_t, gates_t, tokens, grad_out, grad_out)

    def halves(block):
        flat = block.shape[-1]
        return block[: experts // 2].reshape(half, flat), block[experts // 2 :].reshape(half, flat)

    x_block = swapped(sent_x, experts)
    x_pieces = gathered(*halves(x_block))
    g_block = swapped(sent_g, experts)
    g_own = halves(g_block[:, :, :width])
    g_next = halves(g_block[:, :, width:])
    g_pieces = (
        g_own
        + g_next
        + (moved(g_own[0], 1), moved(g_own[1], 1))
        + (moved(g_next[0], 3), moved(g_next[1], 3))
    )

    product = 2 * rows * hidden * model_width
    piece, narrow = shape((half, width), BF16), shape((rows, hidden), BF16)
    wide = shape((rows, hidden), F32)
    results = pl.pallas_call(
        forward_kernel,
        name="forward",
        in_specs=[SMEM] + [VMEM] * 11,
        out_specs=(VMEM,) * 11,
        out_shape=(piece,) * 8 + (narrow, wide, wide),
        compiler_params=PARAMS,
        cost_estimate=cost(3 * product, 6 * hidden * model_width + 4 * rows * model_width),
    )(quarter, *x_pieces, w_gate, w_up, w_down)
    y_partials, (acts, slope_in, slope) = results[:8], results[8:]
    y_top, y_bottom = scattered(y_partials)
    y_block = swapped(jnp.concatenate([y_top, y_bottom]), experts)

    results = pl.pallas_call(
        backward_kernel,
        name="backward",
        in_specs=[SMEM] + [VMEM] * 13,
        out_specs=(VMEM,) * 10,
        out_shape=(piece,) * 8 + (narrow, narrow),
        compiler_params=PARAMS,
        cost_estimate=cost(3 * product, 6 * hidden * model_width + 4 * rows * model_width),
    )(quarter, *g_pieces, w_gate, w_up, w_down, slope_in, slope)
    r_partials, (d_gate, d_up) = results[:8], results[8:]
    r_top, r_bottom = scattered(r_partials)
    r_block = swapped(jnp.concatenate([r_top, r_bottom]), experts)

    def weight_grads(name, order, pieces, *sides):
        return pl.pallas_call(
            lambda *refs: weight_kernel(order, *refs),
            name=name,
            in_specs=[SMEM] + [VMEM] * (8 + len(sides)),
            out_specs=(VMEM,) * len(sides),
            out_shape=(shape(w_gate.shape, BF16),) * len(sides),
            compiler_params=PARAMS,
            cost_estimate=cost(
                len(sides) * product, 2 * model_width * (rows + len(sides) * hidden)
            ),
        )(quarter, *pieces, *sides)

    (grad_down,) = weight_grads("weights_down", (0, 1, 3, 2), g_pieces, acts)
    grad_gate, grad_up = weight_grads("weights_in", (0, 3, 1, 2), x_pieces, d_gate, d_up)

    packed = pl.pallas_call(
        combine_out_kernel,
        name="combine_out",
        grid_spec=pltpu.PrefetchScalarGridSpec(
            num_scalar_prefetch=1,
            grid=(1,),
            in_specs=[
                pl.BlockSpec((count, chosen), whole),
                pl.BlockSpec((count, chosen), whole),
                pl.BlockSpec((count, width), mine),
                pl.BlockSpec((rows, width), whole),
            ],
            out_specs=pl.BlockSpec((count, width + 128), whole),
        ),
        out_shape=shape((count, width + 128), BF16),
        compiler_params=PARAMS,
    )(quarter, expert_ids, gates, grad_out, y_block.reshape(rows, width))
    back = pl.pallas_call(
        combine_back_kernel,
        name="combine_back",
        out_shape=shape((count, width), BF16),
        compiler_params=PARAMS,
    )(expert_ids, gates, r_block.reshape(rows, width))
    outs = (packed, moved(packed, 1), moved(packed, 3), moved(packed, 2))
    backs = (back, moved(back, 1), moved(back, 3), moved(back, 2))
    layer_out, gate_grads, token_grads = pl.pallas_call(
        finish_kernel,
        name="finish",
        in_specs=[SMEM] + [VMEM] * 8,
        out_specs=(VMEM,) * 3,
        out_shape=(
            shape((count, model_width), BF16),
            shape((count, chosen), F32),
            shape((count, model_width), BF16),
        ),
        compiler_params=PARAMS,
    )(quarter, *outs, *backs)
    return layer_out, gate_grads, token_grads, grad_gate, grad_up, grad_down


def solution(mesh):
    rows, cut = P("ep", None), P("ep", "tp", None)
    return jax.shard_map(
        on_device,
        mesh=mesh,
        in_specs=(rows, rows, rows, cut, cut, cut, rows),
        out_specs=(rows, rows, rows, cut, cut, cut),
        check_vma=False,
    )
```

```python
import functools

import jax
import jax.numpy as jnp
from jax import lax
from jax.experimental import pallas as pl
from jax.experimental.pallas import tpu as pltpu
from jax.sharding import PartitionSpec as P

SLOTS = 4
BLOCK = 2 * SLOTS
AHEAD_IN = (0, 3, 1, 2)
AHEAD_OUT = (2, 1, 3, 0)
NN = (((1,), (0,)), ((), ()))
NT = (((1,), (1,)), ((), ()))
TN = (((0,), (0,)), ((), ()))
F32 = jnp.float32
BF16 = jnp.bfloat16
ANY = pl.BlockSpec(memory_space=pl.ANY)
PARAMS = pltpu.CompilerParams(vmem_limit_bytes=56 * 1024 * 1024)


def dot(left, right, dims=NN):
    return lax.dot_general(left, right, dims, preferred_element_type=F32)


def cost(flops, moved):
    return pl.CostEstimate(flops=flops, bytes_accessed=moved, transcendentals=0)


def row_facts(shape, dim):
    row = lax.broadcasted_iota(jnp.int32, shape, dim)
    second = lax.rem(lax.div(row, SLOTS), 2) == 1
    return lax.div(row, BLOCK), lax.rem(row, SLOTS).astype(F32), second


def picks_by_token(ids_ref, gates_ref, row_count):
    count, chosen = ids_ref.shape
    shape = (count, row_count)
    expert, slot, second = row_facts(shape, 1)
    hits = [ids_ref[:, k : k + 1] == expert for k in range(chosen)]
    named = jnp.zeros(shape, F32)
    gate = jnp.zeros(shape, F32)
    for k in range(chosen):
        named = named + jnp.where(hits[k], 1.0, 0.0)
        gate = gate + jnp.where(hits[k], gates_ref[:, k : k + 1], 0.0)
    rows = lax.broadcasted_iota(jnp.int32, (count, count), 0)
    earlier = jnp.where(lax.broadcasted_iota(jnp.int32, (count, count), 1) < rows, 1.0, 0.0)
    before = dot(earlier.astype(BF16), named.astype(BF16))
    pick = jnp.where(before == slot, named, 0.0)
    return pick, gate, hits, second


def dispatch_kernel(quarter, ids_ref, gates_ref, tok_ref, dy_ref, x_ref, g_ref):
    chosen, count = ids_ref.shape
    half = x_ref.shape[1]
    shape = (x_ref.shape[0], count)
    expert, slot, second = row_facts(shape, 0)
    named = jnp.zeros(shape, F32)
    gate = jnp.zeros(shape, F32)
    for k in range(chosen):
        hit = ids_ref[k : k + 1, :] == expert
        named = named + jnp.where(hit, 1.0, 0.0)
        gate = gate + jnp.where(hit, gates_ref[k : k + 1, :], 0.0)
    cols = lax.broadcasted_iota(jnp.int32, (count, count), 1)
    earlier = jnp.where(lax.broadcasted_iota(jnp.int32, (count, count), 0) < cols, 1.0, 0.0)
    before = dot(named.astype(BF16), earlier.astype(BF16))
    pick = jnp.where(before == slot, named, 0.0)
    scale = jnp.sum(pick * gate, axis=1, keepdims=True)
    low = jnp.where(second, 0.0, pick).astype(BF16)
    high = jnp.where(second, pick, 0.0).astype(BF16)
    x_ref[...] = (dot(low, tok_ref[:, 0:half]) + dot(high, tok_ref[:, half:])).astype(BF16)
    g_rows = dot(low, dy_ref[:, 0:half]) + dot(high, dy_ref[:, half:])
    g_ref[...] = (scale * g_rows).astype(BF16)


def expert_kernel(middle, ins, quarter, *refs):
    pieces, refs = refs[:7], refs[7:]
    in_refs, refs = refs[:ins], refs[ins:]
    out_weights, refs = refs[: 3 - ins], refs[3 - ins :]
    extra = 0 if ins == 2 else 2
    extras, refs = refs[:extra], refs[extra:]
    outs, all_ref, kept, (gathered, sums, pre, back, in_sem, out_sem) = refs[:7], refs[7], refs[8:-6], refs[-6:]
    step = pl.program_id(0)
    rows, half = gathered.shape[1:]
    top, bottom = pl.ds(0, rows // 2), pl.ds(rows // 2, rows // 2)
    places = [gathered.at[0]] + [gathered.at[j, span] for j in (1, 2, 3) for span in (top, bottom)]
    loads = [
        pltpu.make_async_copy(piece, place, in_sem.at[n])
        for n, (piece, place) in enumerate(zip(pieces, places))
    ]
    places = [sums.at[j, span] for j in (0, 1, 2) for span in (top, bottom)] + [sums.at[3]]
    stores = [
        pltpu.make_async_copy(place, out, out_sem.at[n])
        for n, (place, out) in enumerate(zip(places, outs))
    ]
    stores.append(pltpu.make_async_copy(gathered, all_ref, out_sem.at[7]))
    groups = ((0,), (1, 2), (3, 4), (5, 6))

    @pl.when(step == 0)
    def _():
        for load in loads:
            load.start()
        pre[...] = jnp.zeros_like(pre)

    for j in range(4):

        @pl.when(step == j)
        def _():
            for n in groups[j]:
                loads[n].wait()

    @pl.when(step < 4)
    def _():
        block = gathered[step]
        for m, w_ref in enumerate(in_refs):
            pre[2 * m] += dot(block, w_ref[:, 0:half], NT)
            pre[2 * m + 1] += dot(block, w_ref[:, half:], NT)

    @pl.when(step == 4)
    def _():
        stores[7].start()
        second = row_facts(pre.shape[1:], 0)[2]
        firsts = [pre[2 * m] + pltpu.roll(pre[2 * m + 1], rows - SLOTS, 0) for m in range(ins)]
        results = middle(firsts, extras, kept)
        for m, value in enumerate(results):
            value = jnp.where(second, 0.0, value)
            back[2 * m] = value.astype(BF16)
            back[2 * m + 1] = pltpu.roll(value, SLOTS, 0).astype(BF16)
        kept[0][...] = back[...]

    @pl.when(step >= 4)
    def _():
        total = None
        for m, w_ref in enumerate(out_weights):
            new = dot(back[2 * m], w_ref[:, 0:half]), dot(back[2 * m + 1], w_ref[:, half:])
            total = new if total is None else (total[0] + new[0], total[1] + new[1])
        sums[step - 4] = (total[0] + total[1]).astype(BF16)

    for j in range(4):

        @pl.when(step == 4 + j)
        def _():
            for n in (2 * j, 2 * j + 1) if j < 3 else (6,):
                stores[n].start()

    @pl.when(step == 7)
    def _():
        for store in stores:
            store.wait()


def forward_middle(firsts, extras, kept):
    a, b = firsts
    sig = jax.nn.sigmoid(a)
    act = a * sig
    kept[1][...] = act
    kept[2][...] = b * sig * (1.0 + a * (1.0 - sig))
    return (act * b,)


def backward_middle(firsts, extras, kept):
    act_ref, slope_ref = extras
    return firsts[0] * slope_ref[...], firsts[0] * act_ref[...]


def weight_kernel(quarter, x_ref, g_ref, h_ref, d_ref, gate_ref, up_ref, down_ref):
    half = x_ref.shape[-1]
    x_rows, g_rows = x_ref[0], g_ref[0]
    for out_ref, acts, n, rows in (
        (gate_ref, d_ref, 0, x_rows),
        (up_ref, d_ref, 2, x_rows),
        (down_ref, h_ref, 0, g_rows),
    ):
        out_ref[:, 0:half] = dot(acts[n], rows, TN).astype(BF16)
        out_ref[:, half:] = dot(acts[n + 1], rows, TN).astype(BF16)


def combine_out_kernel(quarter, ids_ref, gates_ref, dy_ref, rows_ref, out_ref):
    count, chosen = ids_ref.shape
    width = dy_ref.shape[1]
    half = width // 2
    rows = rows_ref[...]
    pick, gate, hits, second = picks_by_token(ids_ref, gates_ref, rows.shape[0])
    products = jnp.zeros_like(pick)
    for h in range(2):
        span = slice(h * half, (h + 1) * half)
        mine = jnp.where(second == (h == 1), pick, 0.0)
        weight = mine * gate
        high = weight.astype(BF16)
        low = (weight - high.astype(F32)).astype(BF16)
        out_ref[:, span] = (dot(high, rows) + dot(low, rows)).astype(BF16)
        products = products + mine * dot(dy_ref[:, span], rows, NT)
    lane = lax.broadcasted_iota(jnp.int32, (count, 128), 1)
    share = jnp.zeros((count, 128), F32)
    for k in range(chosen):
        value = jnp.sum(jnp.where(hits[k], products, 0.0), axis=1, keepdims=True)
        share = share + jnp.where(lax.rem(lane, chosen) == k, value, 0.0)
    first = share.astype(BF16).astype(F32)
    rest = share - first
    middle = rest.astype(BF16).astype(F32)
    parts = jnp.where(lane < chosen, first, jnp.where(lane < 2 * chosen, middle, rest - middle))
    out_ref[:, width : width + 128] = parts.astype(BF16)


def combine_back_kernel(ids_ref, gates_ref, rows_ref, out_ref):
    half = rows_ref.shape[1]
    rows = rows_ref[...]
    pick, _, _, second = picks_by_token(ids_ref, gates_ref, rows.shape[0])
    for h in range(2):
        mine = jnp.where(second == (h == 1), pick, 0.0).astype(BF16)
        out_ref[:, h * half : (h + 1) * half] = dot(mine, rows).astype(BF16)


def finish_kernel(q_ref, *refs):
    outs, backs, (layer_ref, gate_ref, token_ref) = refs[:4], refs[4:8], refs[8:]
    count, chosen = gate_ref.shape
    width = backs[0].shape[1]
    share = jnp.zeros((count, 128), F32)
    for j, ahead in enumerate(AHEAD_IN):
        span = pl.ds(pl.multiple_of(lax.rem(q_ref[0] + ahead, 4) * width, width), width)
        layer_ref[:, span] = outs[j][:, 0:width]
        token_ref[:, span] = backs[j][...]
        share = share + outs[j][:, width : width + 128].astype(F32)
    total = share[:, 0:chosen]
    for j in range(1, 3):
        total = total + share[:, j * chosen : (j + 1) * chosen]
    gate_ref[...] = total


def sum_kernel(own_ref, left_t, right_t, left_b, right_b, out_ref):
    half = left_t.shape[0]
    for span, left_ref, right_ref in (
        (slice(0, half), left_t, right_t),
        (slice(half, 2 * half), left_b, right_b),
    ):
        value = own_ref[span, :].astype(F32) + left_ref[...].astype(F32) + right_ref[...].astype(F32)
        out_ref[span, :] = value.astype(BF16)


def moved(value, ahead):
    return lax.ppermute(value, "tp", [(i, (i + ahead) % 4) for i in range(4)])


def ring_gathered(own):
    half = own.shape[0] // 2
    top, bottom = own[:half], own[half:]
    left_t, right_b = moved(top, 1), moved(bottom, 3)
    left_b, right_t = moved(bottom, 1), moved(top, 3)
    far_t, far_b = moved(left_t, 1), moved(right_b, 3)
    return own, left_t, left_b, right_t, right_b, far_t, far_b


def added(a, b):
    return (a.astype(F32) + b.astype(F32)).astype(BF16)


def after(value, other):
    return lax.optimization_barrier((value, other))[0]


def ring_summed(partials, gate=None):
    far_t, far_b, right_t, right_b, left_t, left_b, own = partials
    in_t, in_b = moved(far_t, 1), moved(far_b, 3)
    from_left_b, from_right_t = moved(right_b, 1), moved(left_t, 3)
    if gate is not None:
        right_t, left_b = after(right_t, gate), after(left_b, gate)
    from_left_t = moved(added(right_t, in_t), 1)
    from_right_b = moved(added(left_b, in_b), 3)
    return pl.pallas_call(
        sum_kernel,
        name="sum",
        out_shape=jax.ShapeDtypeStruct(own.shape, BF16),
        compiler_params=SMALL,
    )(own, from_left_t, from_right_t, from_left_b, from_right_b)


SMALL = pltpu.CompilerParams(vmem_limit_bytes=16 * 1024 * 1024)


def swapped(rows, experts):
    block = rows.reshape(experts, BLOCK, rows.shape[-1])
    return lax.all_to_all(block, "ep", 0, 0, tiled=True).reshape(rows.shape)


def ahead_at(step, table):
    value = jnp.int32(table[3])
    for j in range(3):
        value = jnp.where(step == j, table[j], value)
    return value


def on_device(tokens, expert_ids, gates, w_gate, w_up, w_down, grad_out):
    count, model_width = tokens.shape
    chosen = expert_ids.shape[1]
    hidden = w_gate.shape[1]
    experts = lax.axis_size("ep")
    width = model_width // 4
    rows, half = experts * BLOCK, width // 2
    quarter = lax.axis_index("tp").astype(jnp.int32).reshape(1)
    shape = jax.ShapeDtypeStruct

    whole = lambda i, q: (0, 0)
    mine = lambda i, q: (0, q[0])
    sent_x, sent_g = pl.pallas_call(
        dispatch_kernel,
        name="dispatch",
        grid_spec=pltpu.PrefetchScalarGridSpec(
            num_scalar_prefetch=1,
            grid=(1,),
            in_specs=[
                pl.BlockSpec((chosen, count), whole),
                pl.BlockSpec((chosen, count), whole),
                pl.BlockSpec((count, width), mine),
                pl.BlockSpec((count, width), mine),
            ],
            out_specs=(pl.BlockSpec((rows, half), whole),) * 2,
        ),
        out_shape=(shape((rows, half), BF16),) * 2,
        compiler_params=pltpu.CompilerParams(vmem_limit_bytes=60 * 1024 * 1024),
    )(quarter, expert_ids.T, gates.T, tokens, grad_out)

    x_own = swapped(sent_x, experts)
    sent_g = after(sent_g, x_own)
    x_pieces = ring_gathered(x_own)
    g_own = swapped(sent_g, experts)
    g_pieces = ring_gathered(g_own)

    product = 2 * rows * hidden * model_width
    first = lambda i, q: (0, 0, lax.rem(q[0] + ahead_at(jnp.minimum(i, 3), AHEAD_IN), 4))
    last = lambda i, q: (0, 0, lax.rem(q[0] + ahead_at(jnp.maximum(i - 4, 0), AHEAD_OUT), 4))
    all3 = lambda i, q: (0, 0, 0)
    half_piece = shape((rows // 2, half), BF16)
    wide = pl.BlockSpec((rows, hidden), whole)

    def expert_call(name, middle, pieces, ins, out_weights, extras, wides):
        backs = 2 * len(out_weights)
        return pl.pallas_call(
            functools.partial(expert_kernel, middle, len(ins)),
            name=name,
            grid_spec=pltpu.PrefetchScalarGridSpec(
                num_scalar_prefetch=1,
                grid=(8,),
                in_specs=[ANY] * 7
                + [pl.BlockSpec((None, hidden, width), first)] * len(ins)
                + [pl.BlockSpec((None, hidden, width), last)] * len(out_weights)
                + [wide] * len(extras),
                out_specs=(ANY,) * 8
                + (pl.BlockSpec((backs, rows, hidden), all3),)
                + (wide,) * wides,
                scratch_shapes=[
                    pltpu.VMEM((4, rows, half), BF16),
                    pltpu.VMEM((4, rows, half), BF16),
                    pltpu.VMEM((2 * len(ins), rows, hidden), F32),
                    pltpu.VMEM((backs, rows, hidden), BF16),
                    pltpu.SemaphoreType.DMA((7,)),
                    pltpu.SemaphoreType.DMA((8,)),
                ],
            ),
            out_shape=(half_piece,) * 6
            + (
                shape((rows, half), BF16),
                shape((4, rows, half), BF16),
                shape((backs, rows, hidden), BF16),
            )
            + (shape((rows, hidden), F32),) * wides,
            compiler_params=PARAMS,
            cost_estimate=cost(3 * product, 6 * hidden * model_width + 6 * rows * half * 4),
        )(quarter, *pieces, *ins, *out_weights, *extras)

    results = expert_call("forward", forward_middle, x_pieces, (w_gate, w_up), (w_down,), (), 2)
    y_partials, (x_all, hiddens, act, slope) = results[:7], results[7:]
    y_rows = swapped(ring_summed(y_partials, g_own), experts)
    results = expert_call(
        "backward", backward_middle, g_pieces, (w_down,), (w_gate, w_up), (act, slope), 0
    )
    r_partials, (g_all, grads) = results[:7], results[7:]
    r_rows = swapped(ring_summed(r_partials), experts)

    block = pl.BlockSpec((1, rows, half), lambda i, q: (i, 0, 0))
    grad_block = pl.BlockSpec(
        (None, hidden, width), lambda i, q: (0, 0, lax.rem(q[0] + ahead_at(i, AHEAD_IN), 4))
    )
    grad_gate, grad_up, grad_down = pl.pallas_call(
        weight_kernel,
        name="weights",
        grid_spec=pltpu.PrefetchScalarGridSpec(
            num_scalar_prefetch=1,
            grid=(4,),
            in_specs=[
                block,
                block,
                pl.BlockSpec((2, rows, hidden), all3),
                pl.BlockSpec((4, rows, hidden), all3),
            ],
            out_specs=(grad_block,) * 3,
        ),
        out_shape=(shape(w_gate.shape, BF16),) * 3,
        compiler_params=PARAMS,
        cost_estimate=cost(3 * product, 2 * model_width * (rows + 3 * hidden)),
    )(quarter, x_all, g_all, hiddens, grads)

    packed = pl.pallas_call(
        combine_out_kernel,
        name="combine_out",
        grid_spec=pltpu.PrefetchScalarGridSpec(
            num_scalar_prefetch=1,
            grid=(1,),
            in_specs=[
                pl.BlockSpec((count, chosen), whole),
                pl.BlockSpec((count, chosen), whole),
                pl.BlockSpec((count, width), mine),
                pl.BlockSpec((rows, half), whole),
            ],
            out_specs=pl.BlockSpec((count, width + 128), whole),
        ),
        out_shape=shape((count, width + 128), BF16),
        compiler_params=SMALL,
    )(quarter, expert_ids, gates, grad_out, y_rows)
    back = pl.pallas_call(
        combine_back_kernel,
        name="combine_back",
        out_shape=shape((count, width), BF16),
        compiler_params=SMALL,
    )(expert_ids, gates, r_rows)
    outs = (packed, moved(packed, 1), moved(packed, 3), moved(packed, 2))
    backs = (back, moved(back, 1), moved(back, 3), moved(back, 2))
    vmem, smem = pl.BlockSpec(memory_space=pltpu.VMEM), pl.BlockSpec(memory_space=pltpu.SMEM)
    layer_out, gate_grads, token_grads = pl.pallas_call(
        finish_kernel,
        name="finish",
        in_specs=[smem] + [vmem] * 8,
        out_specs=(vmem,) * 3,
        out_shape=(
            shape((count, model_width), BF16),
            shape((count, chosen), F32),
            shape((count, model_width), BF16),
        ),
        compiler_params=SMALL,
    )(quarter, *outs, *backs)
    return layer_out, gate_grads, token_grads, grad_gate, grad_up, grad_down


def solution(mesh):
    rows, cut = P("ep", None), P("ep", "tp", None)
    return jax.shard_map(
        on_device,
        mesh=mesh,
        in_specs=(rows, rows, rows, cut, cut, cut, rows),
        out_specs=(rows, rows, rows, cut, cut, cut),
        check_vma=False,
    )
```

```python
import functools

import jax
import jax.numpy as jnp
from jax import lax
from jax.experimental import pallas as pl
from jax.experimental.pallas import tpu as pltpu
from jax.sharding import PartitionSpec as P

SLOTS = 4
BLOCK = 2 * SLOTS
AHEAD_IN = (0, 3, 1, 2)
AHEAD_OUT = (2, 1, 3, 0)
NN = (((1,), (0,)), ((), ()))
NT = (((1,), (1,)), ((), ()))
TN = (((0,), (0,)), ((), ()))
F32 = jnp.float32
BF16 = jnp.bfloat16
ANY = pl.BlockSpec(memory_space=pl.ANY)
PARAMS = pltpu.CompilerParams(vmem_limit_bytes=56 * 1024 * 1024)


def dot(left, right, dims=NN):
    return lax.dot_general(left, right, dims, preferred_element_type=F32)


def cost(flops, moved):
    return pl.CostEstimate(flops=flops, bytes_accessed=moved, transcendentals=0)


def row_facts(shape, dim):
    row = lax.broadcasted_iota(jnp.int32, shape, dim)
    second = lax.rem(lax.div(row, SLOTS), 2) == 1
    return lax.div(row, BLOCK), lax.rem(row, SLOTS).astype(F32), second


def picks_by_token(ids_ref, gates_ref, row_count):
    count, chosen = ids_ref.shape
    shape = (count, row_count)
    expert, slot, second = row_facts(shape, 1)
    hits = [ids_ref[:, k : k + 1] == expert for k in range(chosen)]
    named = jnp.zeros(shape, F32)
    gate = jnp.zeros(shape, F32)
    for k in range(chosen):
        named = named + jnp.where(hits[k], 1.0, 0.0)
        gate = gate + jnp.where(hits[k], gates_ref[:, k : k + 1], 0.0)
    rows = lax.broadcasted_iota(jnp.int32, (count, count), 0)
    earlier = jnp.where(lax.broadcasted_iota(jnp.int32, (count, count), 1) < rows, 1.0, 0.0)
    before = dot(earlier.astype(BF16), named.astype(BF16))
    pick = jnp.where(before == slot, named, 0.0)
    return pick, gate, hits, second


def dispatch_kernel(quarter, ids_ref, gates_ref, tok_ref, dy_ref, x_ref, g_ref):
    chosen, count = ids_ref.shape
    half = x_ref.shape[1]
    shape = (x_ref.shape[0], count)
    expert, slot, second = row_facts(shape, 0)
    named = jnp.zeros(shape, F32)
    gate = jnp.zeros(shape, F32)
    for k in range(chosen):
        hit = ids_ref[k : k + 1, :] == expert
        named = named + jnp.where(hit, 1.0, 0.0)
        gate = gate + jnp.where(hit, gates_ref[k : k + 1, :], 0.0)
    cols = lax.broadcasted_iota(jnp.int32, (count, count), 1)
    earlier = jnp.where(lax.broadcasted_iota(jnp.int32, (count, count), 0) < cols, 1.0, 0.0)
    before = dot(named.astype(BF16), earlier.astype(BF16))
    pick = jnp.where(before == slot, named, 0.0)
    scale = jnp.sum(pick * gate, axis=1, keepdims=True)
    low = jnp.where(second, 0.0, pick).astype(BF16)
    high = jnp.where(second, pick, 0.0).astype(BF16)
    x_ref[...] = (dot(low, tok_ref[:, 0:half]) + dot(high, tok_ref[:, half:])).astype(BF16)
    g_rows = dot(low, dy_ref[:, 0:half]) + dot(high, dy_ref[:, half:])
    g_ref[...] = (scale * g_rows).astype(BF16)


def spread(q_ref, place, ahead, width):
    start = lax.rem(q_ref[0] + ahead, 4) * width + place * (width // 2)
    return pl.ds(pl.multiple_of(start, width // 2), width // 2)


def expert_kernel(middle, forward, extra, q_ref, *refs):
    pieces, (wg_ref, wu_ref, wd_ref), refs = refs[:5], refs[5:8], refs[8:]
    extras, refs = refs[:extra], refs[extra:]
    outs, all_ref, kept = refs[:5], refs[5], refs[6:-5]
    gathered, sums, inner, outer, sems = refs[-5:]
    rows, half = sums.shape[1:]
    hidden = wd_ref.shape[1]
    width = 2 * half
    ups, downs = (inner, outer) if forward else (outer, inner)
    top, bottom = slice(0, rows // 2), slice(rows // 2, rows)
    spots = [(slice(0, rows), j) for j in range(3)] + [(top, 3), (bottom, 3)]
    count = iter(range(64))

    def copy(source, target):
        return pltpu.make_async_copy(source, target, sems.at[next(count)])

    loads = [
        copy(piece, gathered.at[span, j * half : (j + 1) * half])
        for piece, (span, j) in zip(pieces, spots)
    ]
    up_loads, down_loads = [], []
    for j in range(4):
        for h in range(2):
            for n, w_ref in ((0, wg_ref), (1, wu_ref)):
                place = (2 * h + n) * hidden
                ahead = AHEAD_IN[j] if forward else AHEAD_OUT[j]
                up_loads.append(
                    copy(
                        w_ref.at[0, :, spread(q_ref, h, ahead, width)],
                        ups.at[place : place + hidden, j * half : (j + 1) * half],
                    )
                )
            ahead = AHEAD_OUT[j] if forward else AHEAD_IN[j]
            down_loads.append(
                copy(
                    wd_ref.at[0, :, spread(q_ref, h, ahead, width)],
                    downs.at[h * hidden : (h + 1) * hidden, j * half : (j + 1) * half],
                )
            )
    first_loads, last_loads = (up_loads, down_loads) if forward else (down_loads, up_loads)
    for load in loads + first_loads + last_loads:
        load.start()
    for load in loads + first_loads:
        load.wait()
    saved = copy(gathered, all_ref)
    saved.start()
    both = dot(gathered[...], inner[...], NT)
    split = both.shape[1] // 2
    first = both[:, :split] + pltpu.roll(both[:, split:], rows - SLOTS, 0)
    value = middle(first, extras, kept)
    value = jnp.where(row_facts(value.shape, 0)[2], 0.0, value)
    split = value.shape[1]
    kept[0][:, :split] = value.astype(BF16)
    kept[0][:, split:] = pltpu.roll(value, SLOTS, 0).astype(BF16)
    for load in last_loads:
        load.wait()
    stores = []
    for j in range(4):
        sums[j] = dot(kept[0][...], outer[:, j * half : (j + 1) * half]).astype(BF16)
        if j == 0:
            stores.append(copy(sums.at[0, top], outs[0]))
            stores[-1].start()
        stores.append(copy(sums.at[0, bottom] if j == 0 else sums.at[j], outs[j + 1]))
        stores[-1].start()
    for store in stores + [saved]:
        store.wait()


def forward_middle(first, extras, kept):
    hidden = first.shape[1] // 2
    a, b = first[:, :hidden], first[:, hidden:]
    sig = jax.nn.sigmoid(a)
    act = a * sig
    kept[1][:, :hidden] = b * sig * (1.0 + a * (1.0 - sig))
    kept[1][:, hidden:] = act
    return act * b


def backward_middle(first, extras, kept):
    return jnp.concatenate([first, first], axis=1) * extras[0][...]


def weight_kernel(quarter, x_ref, g_ref, h_ref, d_ref, gate_ref, up_ref, down_ref):
    half = x_ref.shape[-1]
    hidden = gate_ref.shape[0]
    inside = dot(d_ref[...], x_ref[...], TN).astype(BF16)
    outside = dot(h_ref[...], g_ref[...], TN).astype(BF16)
    for h in range(2):
        span = slice(h * half, (h + 1) * half)
        gate_ref[:, span] = inside[2 * h * hidden : (2 * h + 1) * hidden]
        up_ref[:, span] = inside[(2 * h + 1) * hidden : (2 * h + 2) * hidden]
        down_ref[:, span] = outside[h * hidden : (h + 1) * hidden]


def combine_kernel(quarter, ids_ref, gates_ref, dy_ref, rows_ref, out_ref):
    count, chosen = ids_ref.shape
    width = dy_ref.shape[1]
    half = width // 2
    y_rows, r_rows = rows_ref[:, 0:half], rows_ref[:, half:]
    pick, gate, hits, second = picks_by_token(ids_ref, gates_ref, y_rows.shape[0])
    products = jnp.zeros_like(pick)
    for h in range(2):
        span = slice(h * half, (h + 1) * half)
        mine = jnp.where(second == (h == 1), pick, 0.0)
        weight = mine * gate
        high = weight.astype(BF16)
        low = (weight - high.astype(F32)).astype(BF16)
        out_ref[0:count, span] = (dot(high, y_rows) + dot(low, y_rows)).astype(BF16)
        out_ref[count : 2 * count, span] = dot(mine.astype(BF16), r_rows).astype(BF16)
        products = products + mine * dot(dy_ref[:, span], y_rows, NT)
    lane = lax.broadcasted_iota(jnp.int32, (count, 128), 1)
    share = jnp.zeros((count, 128), F32)
    for k in range(chosen):
        value = jnp.sum(jnp.where(hits[k], products, 0.0), axis=1, keepdims=True)
        share = share + jnp.where(lax.rem(lane, chosen) == k, value, 0.0)
    first = share.astype(BF16).astype(F32)
    rest = share - first
    middle = rest.astype(BF16).astype(F32)
    parts = jnp.where(lane < chosen, first, jnp.where(lane < 2 * chosen, middle, rest - middle))
    out_ref[0:count, width : width + 128] = parts.astype(BF16)
    out_ref[count : 2 * count, width : width + 128] = jnp.zeros((count, 128), BF16)


def finish_kernel(q_ref, *refs):
    pieces, (layer_ref, gate_ref, token_ref) = refs[:4], refs[4:]
    count, chosen = gate_ref.shape
    width = layer_ref.shape[1] // 4
    share = jnp.zeros((count, 128), F32)
    for j, ahead in enumerate(AHEAD_IN):
        span = pl.ds(pl.multiple_of(lax.rem(q_ref[0] + ahead, 4) * width, width), width)
        layer_ref[:, span] = pieces[j][0:count, 0:width]
        token_ref[:, span] = pieces[j][count : 2 * count, 0:width]
        share = share + pieces[j][0:count, width : width + 128].astype(F32)
    total = share[:, 0:chosen]
    for j in range(1, 3):
        total = total + share[:, j * chosen : (j + 1) * chosen]
    gate_ref[...] = total


def sum_kernel(*refs):
    inputs, out_ref = refs[:-1], refs[-1]
    width = out_ref.shape[1] // 2
    for n in range(2):
        value = inputs[3 * n][...].astype(F32)
        for ref in inputs[3 * n + 1 : 3 * n + 3]:
            value = value + ref[...].astype(F32)
        out_ref[:, n * width : (n + 1) * width] = value.astype(BF16)


def moved(value, ahead):
    return lax.ppermute(value, "tp", [(i, (i + ahead) % 4) for i in range(4)])


def ring_gathered(own):
    half = own.shape[0] // 2
    left, right = moved(own, 1), moved(own, 3)
    far_t, far_b = moved(left[:half], 1), moved(right[half:], 3)
    return own, left, right, far_t, far_b


def added(a, b):
    return (a.astype(F32) + b.astype(F32)).astype(BF16)


def after(value, other):
    return lax.optimization_barrier((value, other))[0]


def ring_terms(partials):
    far_t, far_b, right, left, own = partials
    half = far_t.shape[0]
    in_t, in_b = moved(far_t, 1), moved(far_b, 3)
    from_left = moved(jnp.concatenate([added(right[:half], in_t), right[half:]]), 1)
    from_right = moved(jnp.concatenate([left[:half], added(left[half:], in_b)]), 3)
    return own, from_left, from_right


SMALL = pltpu.CompilerParams(vmem_limit_bytes=16 * 1024 * 1024)


def swapped(rows, experts):
    block = rows.reshape(experts, BLOCK, rows.shape[-1])
    return lax.all_to_all(block, "ep", 0, 0, tiled=True).reshape(rows.shape)


def ahead_at(step, table):
    value = jnp.int32(table[3])
    for j in range(3):
        value = jnp.where(step == j, table[j], value)
    return value


def on_device(tokens, expert_ids, gates, w_gate, w_up, w_down, grad_out):
    count, model_width = tokens.shape
    chosen = expert_ids.shape[1]
    hidden = w_gate.shape[1]
    experts = lax.axis_size("ep")
    width = model_width // 4
    rows, half = experts * BLOCK, width // 2
    quarter = lax.axis_index("tp").astype(jnp.int32).reshape(1)
    shape = jax.ShapeDtypeStruct

    whole = lambda i, q: (0, 0)
    mine = lambda i, q: (0, q[0])
    sent_x, sent_g = pl.pallas_call(
        dispatch_kernel,
        name="dispatch",
        grid_spec=pltpu.PrefetchScalarGridSpec(
            num_scalar_prefetch=1,
            grid=(1,),
            in_specs=[
                pl.BlockSpec((chosen, count), whole),
                pl.BlockSpec((chosen, count), whole),
                pl.BlockSpec((count, width), mine),
                pl.BlockSpec((count, width), mine),
            ],
            out_specs=(pl.BlockSpec((rows, half), whole),) * 2,
        ),
        out_shape=(shape((rows, half), BF16),) * 2,
        compiler_params=pltpu.CompilerParams(vmem_limit_bytes=60 * 1024 * 1024),
    )(quarter, expert_ids.T, gates.T, tokens, grad_out)

    x_own = swapped(sent_x, experts)
    sent_g = after(sent_g, x_own)
    x_pieces = ring_gathered(x_own)
    first_pieces = x_pieces[:-1]
    g_own = swapped(sent_g, experts)
    g_pieces = ring_gathered(g_own)

    product = 2 * rows * hidden * model_width
    vmem, smem = pl.BlockSpec(memory_space=pltpu.VMEM), pl.BlockSpec(memory_space=pltpu.SMEM)

    def expert_call(name, middle, forward, pieces, extras):
        ups, downs = pltpu.VMEM((4 * hidden, 4 * half), BF16), pltpu.VMEM((2 * hidden, 4 * half), BF16)
        saved = shape((rows, 2 * hidden if forward else 4 * hidden), BF16)
        return pl.pallas_call(
            functools.partial(expert_kernel, middle, forward, len(extras)),
            name=name,
            in_specs=[smem] + [ANY] * 8 + [vmem] * len(extras),
            out_specs=(ANY,) * 6 + (vmem,) * (2 if forward else 1),
            scratch_shapes=[
                pltpu.VMEM((rows, 4 * half), BF16),
                pltpu.VMEM((4, rows, half), BF16),
                ups if forward else downs,
                downs if forward else ups,
                pltpu.SemaphoreType.DMA((40,)),
            ],
            out_shape=(shape((rows // 2, half), BF16),) * 2
            + (shape((rows, half), BF16),) * 3
            + (shape((rows, 4 * half), BF16), saved)
            + ((shape((rows, 2 * hidden), F32),) if forward else ()),
            compiler_params=PARAMS,
            cost_estimate=cost(3 * product, 6 * hidden * model_width + 6 * rows * half * 4),
        )(quarter, *pieces, w_gate, w_up, w_down, *extras)

    x_pieces = (after(x_pieces[-1], g_own),)
    results = expert_call("forward", forward_middle, True, first_pieces + x_pieces, ())
    y_partials, (x_all, hiddens, factors) = results[:5], results[5:]
    y_terms = ring_terms(y_partials)
    results = expert_call("backward", backward_middle, False, g_pieces, (factors,))
    r_partials, (g_all, grads) = results[:5], results[5:]
    r_terms = ring_terms(r_partials)
    summed = pl.pallas_call(
        sum_kernel,
        name="sum",
        out_shape=shape((rows, width), BF16),
        compiler_params=SMALL,
    )(*y_terms, *r_terms)
    returned = swapped(summed, experts)

    block = pl.BlockSpec((rows, half), lambda i, q: (0, i))
    grad_block = pl.BlockSpec(
        (None, hidden, width), lambda i, q: (0, 0, lax.rem(q[0] + ahead_at(i, AHEAD_IN), 4))
    )
    grad_gate, grad_up, grad_down = pl.pallas_call(
        weight_kernel,
        name="weights",
        grid_spec=pltpu.PrefetchScalarGridSpec(
            num_scalar_prefetch=1,
            grid=(4,),
            in_specs=[
                block,
                block,
                pl.BlockSpec((rows, 2 * hidden), whole),
                pl.BlockSpec((rows, 4 * hidden), whole),
            ],
            out_specs=(grad_block,) * 3,
        ),
        out_shape=(shape(w_gate.shape, BF16),) * 3,
        compiler_params=PARAMS,
        cost_estimate=cost(3 * product, 2 * model_width * (rows + 3 * hidden)),
    )(quarter, x_all, g_all, hiddens, grads)
    returned = after(returned, grad_down)

    packed = pl.pallas_call(
        combine_kernel,
        name="combine",
        grid_spec=pltpu.PrefetchScalarGridSpec(
            num_scalar_prefetch=1,
            grid=(1,),
            in_specs=[
                pl.BlockSpec((count, chosen), whole),
                pl.BlockSpec((count, chosen), whole),
                pl.BlockSpec((count, width), mine),
                pl.BlockSpec((rows, width), whole),
            ],
            out_specs=pl.BlockSpec((2 * count, width + 128), whole),
        ),
        out_shape=shape((2 * count, width + 128), BF16),
        compiler_params=SMALL,
    )(quarter, expert_ids, gates, grad_out, returned)
    layer_out, gate_grads, token_grads = pl.pallas_call(
        finish_kernel,
        name="finish",
        in_specs=[smem] + [vmem] * 4,
        out_specs=(vmem,) * 3,
        out_shape=(
            shape((count, model_width), BF16),
            shape((count, chosen), F32),
            shape((count, model_width), BF16),
        ),
        compiler_params=SMALL,
    )(quarter, packed, moved(packed, 1), moved(packed, 3), moved(packed, 2))
    return layer_out, gate_grads, token_grads, grad_gate, grad_up, grad_down


def solution(mesh):
    rows, cut = P("ep", None), P("ep", "tp", None)
    return jax.shard_map(
        on_device,
        mesh=mesh,
        in_specs=(rows, rows, rows, cut, cut, cut, rows),
        out_specs=(rows, rows, rows, cut, cut, cut),
        check_vma=False,
    )
```

```python
import jax
import jax.numpy as jnp
from jax import lax
from jax.experimental import pallas as pl
from jax.experimental.pallas import tpu as pltpu
from jax.sharding import PartitionSpec as P

SLOTS = 4
BLOCK = 2 * SLOTS
AHEAD_IN = (0, 3, 1, 2)
AHEAD_OUT = (2, 1, 3, 0)
NN = (((1,), (0,)), ((), ()))
NT = (((1,), (1,)), ((), ()))
TN = (((0,), (0,)), ((), ()))
F32 = jnp.float32
BF16 = jnp.bfloat16
ANY = pl.BlockSpec(memory_space=pl.ANY)
VMEM = pl.BlockSpec(memory_space=pltpu.VMEM)
SMEM = pl.BlockSpec(memory_space=pltpu.SMEM)
PARAMS = pltpu.CompilerParams(vmem_limit_bytes=20 * 1024 * 1024)


def dot(left, right, dims=NN):
    return lax.dot_general(left, right, dims, preferred_element_type=F32)


def cost(flops, moved):
    return pl.CostEstimate(flops=flops, bytes_accessed=moved, transcendentals=0)


def row_facts(shape, dim):
    row = lax.broadcasted_iota(jnp.int32, shape, dim)
    second = lax.rem(lax.div(row, SLOTS), 2) == 1
    return lax.div(row, BLOCK), lax.rem(row, SLOTS).astype(F32), second


def dispatch_kernel(quarter, ids_ref, gates_ref, tok_ref, dy_ref, out_ref):
    chosen, count = ids_ref.shape
    shape = (out_ref.shape[0], count)
    expert, slot, second = row_facts(shape, 0)
    named = jnp.zeros(shape, F32)
    gate = jnp.zeros(shape, F32)
    for k in range(chosen):
        hit = ids_ref[k : k + 1, :] == expert
        named = named + jnp.where(hit, 1.0, 0.0)
        gate = gate + jnp.where(hit, gates_ref[k : k + 1, :], 0.0)
    cols = lax.broadcasted_iota(jnp.int32, (count, count), 1)
    earlier = jnp.where(lax.broadcasted_iota(jnp.int32, (count, count), 0) < cols, 1.0, 0.0)
    before = dot(named.astype(BF16), earlier.astype(BF16))
    pick = jnp.where(before == slot, named, 0.0)
    scale = jnp.sum(pick * jnp.where(second, gate, 1.0), axis=1, keepdims=True)
    pick_x = jnp.where(second, 0.0, pick).astype(BF16)
    pick_g = jnp.where(second, pick, 0.0).astype(BF16)
    rows = dot(pick_x, tok_ref[...]) + dot(pick_g, dy_ref[...])
    out_ref[...] = (scale * rows).astype(BF16)


def placing(packed, rows, kind, packed_dim):
    shape = (packed, rows) if packed_dim == 0 else (rows, packed)
    far = lax.broadcasted_iota(jnp.int32, shape, packed_dim)
    near = lax.broadcasted_iota(jnp.int32, shape, 1 - packed_dim)
    place = lax.div(near, SLOTS) * BLOCK + kind * SLOTS + lax.rem(near, SLOTS)
    return jnp.where(far == place, 1.0, 0.0).astype(BF16)


def unpack_kernel(in_ref, x_ref, g_ref):
    for kind, out_ref in enumerate((x_ref, g_ref)):
        pick = placing(in_ref.shape[0], out_ref.shape[0], kind, 1)
        out_ref[...] = dot(pick, in_ref[...]).astype(BF16)


def sum_kernel(*refs):
    inputs, out_ref = refs[:-1], refs[-1]
    total = None
    for kind in range(2):
        value = inputs[3 * kind][...].astype(F32)
        for ref in inputs[3 * kind + 1 : 3 * kind + 3]:
            value = value + ref[...].astype(F32)
        pick = placing(out_ref.shape[0], value.shape[0], kind, 0)
        new = dot(pick, value.astype(BF16))
        total = new if total is None else total + new
    out_ref[...] = total.astype(BF16)


def columns(q_ref, ahead, width):
    start = lax.rem(q_ref[0] + ahead, 4) * width
    return pl.ds(pl.multiple_of(start, width), width)


def gather_copies(q_ref, pieces, gathered, sems):
    rows, width = pieces[0].shape
    spans = [slice(0, rows)] * 3 + [slice(0, rows // 2), slice(rows // 2, rows)]
    ahead = AHEAD_IN[:3] + (AHEAD_IN[3],) * 2
    return [
        pltpu.make_async_copy(piece, gathered.at[span, columns(q_ref, a, width)], sems.at[n])
        for n, (piece, span, a) in enumerate(zip(pieces, spans, ahead))
    ]


def store_parts(q_ref, outs, width, product):
    for j, ahead in enumerate(AHEAD_OUT):
        part = product(columns(q_ref, ahead, width)).astype(BF16)
        if j == 0:
            half = part.shape[0] // 2
            outs[0][...] = part[:half]
            outs[1][...] = part[half:]
        else:
            outs[j + 1][...] = part


def forward_kernel(q_ref, *refs):
    pieces, (wg_ref, wu_ref, wd_ref), refs = refs[:5], refs[5:8], refs[8:]
    outs, (x_ref, hidden_ref, act_ref, slope_ref, sems) = refs[:5], refs[5:]
    copies = gather_copies(q_ref, pieces, x_ref, sems)
    for copy in copies:
        copy.start()
    for copy in copies:
        copy.wait()
    a = dot(x_ref[...], wg_ref[0], NT)
    b = dot(x_ref[...], wu_ref[0], NT)
    sig = jax.nn.sigmoid(a)
    act = a * sig
    hidden_ref[...] = (act * b).astype(BF16)
    act_ref[...] = act
    slope_ref[...] = b * sig * (1.0 + a * (1.0 - sig))
    store_parts(
        q_ref, outs, pieces[0].shape[1], lambda span: dot(hidden_ref[...], wd_ref[0, :, span])
    )


def backward_kernel(q_ref, *refs):
    pieces, (wg_ref, wu_ref, wd_ref, act_ref, slope_ref), refs = refs[:5], refs[5:10], refs[10:]
    outs, (g_ref, gate_ref, up_ref, sems) = refs[:5], refs[5:]
    copies = gather_copies(q_ref, pieces, g_ref, sems)
    for copy in copies:
        copy.start()
    for copy in copies:
        copy.wait()
    dh = dot(g_ref[...], wd_ref[0], NT)
    gate_ref[...] = (dh * slope_ref[...]).astype(BF16)
    up_ref[...] = (dh * act_ref[...]).astype(BF16)
    store_parts(
        q_ref,
        outs,
        pieces[0].shape[1],
        lambda span: dot(gate_ref[...], wg_ref[0, :, span]) + dot(up_ref[...], wu_ref[0, :, span]),
    )


def weight_kernel(x_ref, g_ref, h_ref, da_ref, du_ref, gate_ref, up_ref, down_ref):
    gate_ref[...] = dot(da_ref[...], x_ref[...], TN).astype(BF16)
    up_ref[...] = dot(du_ref[...], x_ref[...], TN).astype(BF16)
    down_ref[...] = dot(h_ref[...], g_ref[...], TN).astype(BF16)


def combine_kernel(quarter, ids_ref, gates_ref, dy_ref, rows_ref, out_ref):
    count, chosen = ids_ref.shape
    width = dy_ref.shape[1]
    rows = rows_ref[...]
    shape = (count, rows.shape[0])
    expert, slot, second = row_facts(shape, 1)
    hits = [ids_ref[:, k : k + 1] == expert for k in range(chosen)]
    named = jnp.zeros(shape, F32)
    gate = jnp.zeros(shape, F32)
    for k in range(chosen):
        named = named + jnp.where(hits[k], 1.0, 0.0)
        gate = gate + jnp.where(hits[k], gates_ref[:, k : k + 1], 0.0)
    earlier = lax.broadcasted_iota(jnp.int32, (count, count), 1) < lax.broadcasted_iota(
        jnp.int32, (count, count), 0
    )
    before = dot(jnp.where(earlier, 1.0, 0.0).astype(BF16), named.astype(BF16))
    pick = jnp.where(before == slot, named, 0.0)
    pick_y = jnp.where(second, 0.0, pick)
    pick_r = jnp.where(second, pick, 0.0).astype(BF16)
    weight = pick_y * gate
    high = weight.astype(BF16)
    low = (weight - high.astype(F32)).astype(BF16)
    out_ref[0:count, 0:width] = (dot(high, rows) + dot(low, rows)).astype(BF16)
    out_ref[count : 2 * count, 0:width] = dot(pick_r, rows).astype(BF16)
    products = pick_y * dot(dy_ref[...], rows, NT)
    lane = lax.broadcasted_iota(jnp.int32, (count, 128), 1)
    share = jnp.zeros((count, 128), F32)
    for k in range(chosen):
        value = jnp.sum(jnp.where(hits[k], products, 0.0), axis=1, keepdims=True)
        share = share + jnp.where(lax.rem(lane, chosen) == k, value, 0.0)
    first = share.astype(BF16).astype(F32)
    rest = share - first
    middle = rest.astype(BF16).astype(F32)
    parts = jnp.where(lane < chosen, first, jnp.where(lane < 2 * chosen, middle, rest - middle))
    out_ref[0:count, width : width + 128] = parts.astype(BF16)
    out_ref[count : 2 * count, width : width + 128] = jnp.zeros((count, 128), BF16)


def finish_kernel(q_ref, *refs):
    pieces, (layer_ref, gate_ref, token_ref) = refs[:4], refs[4:]
    count, chosen = gate_ref.shape
    width = layer_ref.shape[1] // 4
    share = jnp.zeros((count, 128), F32)
    for j, ahead in enumerate(AHEAD_IN):
        span = columns(q_ref, ahead, width)
        layer_ref[:, span] = pieces[j][0:count, 0:width]
        token_ref[:, span] = pieces[j][count : 2 * count, 0:width]
        share = share + pieces[j][0:count, width : width + 128].astype(F32)
    total = share[:, 0:chosen]
    for j in range(1, 3):
        total = total + share[:, j * chosen : (j + 1) * chosen]
    gate_ref[...] = total


def moved(value, ahead):
    return lax.ppermute(value, "tp", [(i, (i + ahead) % 4) for i in range(4)])


def ring_gathered(own):
    half = own.shape[0] // 2
    left, right = moved(own, 1), moved(own, 3)
    far_t, far_b = moved(left[:half], 1), moved(right[half:], 3)
    return own, left, right, far_t, far_b


def added(a, b):
    return (a.astype(F32) + b.astype(F32)).astype(BF16)


def after(value, other):
    return lax.optimization_barrier((value, other))[0]


def ring_terms(partials):
    far_t, far_b, right, left, own = partials
    half = far_t.shape[0]
    in_t, in_b = moved(far_t, 1), moved(far_b, 3)
    from_left = moved(jnp.concatenate([added(right[:half], in_t), right[half:]]), 1)
    from_right = moved(jnp.concatenate([left[:half], added(left[half:], in_b)]), 3)
    return own, from_left, from_right


def swapped(rows, experts):
    block = rows.reshape(experts, BLOCK, rows.shape[-1])
    return lax.all_to_all(block, "ep", 0, 0, tiled=True).reshape(rows.shape)


def on_device(tokens, expert_ids, gates, w_gate, w_up, w_down, grad_out):
    count, model_width = tokens.shape
    chosen = expert_ids.shape[1]
    hidden = w_gate.shape[1]
    experts = lax.axis_size("ep")
    width = model_width // 4
    packed_rows, rows = experts * BLOCK, experts * SLOTS
    quarter = lax.axis_index("tp").astype(jnp.int32).reshape(1)
    shape = jax.ShapeDtypeStruct

    whole = lambda i, q: (0, 0)
    mine = lambda i, q: (0, q[0])
    sent = pl.pallas_call(
        dispatch_kernel,
        name="dispatch",
        grid_spec=pltpu.PrefetchScalarGridSpec(
            num_scalar_prefetch=1,
            grid=(1,),
            in_specs=[
                pl.BlockSpec((chosen, count), whole),
                pl.BlockSpec((chosen, count), whole),
                pl.BlockSpec((count, width), mine),
                pl.BlockSpec((count, width), mine),
            ],
            out_specs=pl.BlockSpec((packed_rows, width), whole),
        ),
        out_shape=shape((packed_rows, width), BF16),
        compiler_params=pltpu.CompilerParams(vmem_limit_bytes=60 * 1024 * 1024),
    )(quarter, expert_ids.T, gates.T, tokens, grad_out)
    piece, part = shape((rows, width), BF16), shape((rows // 2, width), BF16)
    full, narrow, wide = (
        shape((rows, model_width), BF16),
        shape((rows, hidden), BF16),
        shape((rows, hidden), F32),
    )
    x_own, g_own = pl.pallas_call(
        unpack_kernel, name="unpack", out_shape=(piece, piece), compiler_params=PARAMS
    )(swapped(sent, experts))
    x_pieces, g_pieces = ring_gathered(x_own), ring_gathered(g_own)

    product = 2 * rows * hidden * model_width

    def expert_call(name, kernel, pieces, extras, kept):
        return pl.pallas_call(
            kernel,
            name=name,
            in_specs=[SMEM] + [ANY] * 5 + [VMEM] * (3 + len(extras)),
            out_specs=(VMEM,) * (6 + len(kept)),
            scratch_shapes=[pltpu.SemaphoreType.DMA((5,))],
            out_shape=(part, part, piece, piece, piece, full) + kept,
            compiler_params=PARAMS,
            cost_estimate=cost(3 * product, 6 * hidden * model_width + 6 * rows * model_width),
        )(quarter, *pieces, w_gate, w_up, w_down, *extras)

    results = expert_call("forward", forward_kernel, x_pieces, (), (narrow, wide, wide))
    y_partials, (x_all, hiddens, act, slope) = results[:5], results[5:]
    y_terms = ring_terms(y_partials)
    results = expert_call("backward", backward_kernel, g_pieces, (act, slope), (narrow, narrow))
    r_partials, (g_all, d_gate, d_up) = results[:5], results[5:]
    r_terms = ring_terms(r_partials)
    summed = pl.pallas_call(
        sum_kernel, name="sum", out_shape=shape((packed_rows, width), BF16), compiler_params=PARAMS
    )(*y_terms, *r_terms)
    returned = swapped(summed, experts)

    block = pl.BlockSpec((rows, width), lambda i: (0, i))
    side = pl.BlockSpec((rows, hidden), lambda i: (0, 0))
    grad_block = pl.BlockSpec((None, hidden, width), lambda i: (0, 0, i))
    grad_gate, grad_up, grad_down = pl.pallas_call(
        weight_kernel,
        name="weights",
        grid=(4,),
        in_specs=[block, block, side, side, side],
        out_specs=(grad_block,) * 3,
        out_shape=(shape(w_gate.shape, BF16),) * 3,
        compiler_params=PARAMS,
        cost_estimate=cost(3 * product, 2 * model_width * (rows + 3 * hidden)),
    )(x_all, g_all, hiddens, d_gate, d_up)
    returned = after(returned, grad_down)

    packed = pl.pallas_call(
        combine_kernel,
        name="combine",
        grid_spec=pltpu.PrefetchScalarGridSpec(
            num_scalar_prefetch=1,
            grid=(1,),
            in_specs=[
                pl.BlockSpec((count, chosen), whole),
                pl.BlockSpec((count, chosen), whole),
                pl.BlockSpec((count, width), mine),
                pl.BlockSpec((packed_rows, width), whole),
            ],
            out_specs=pl.BlockSpec((2 * count, width + 128), whole),
        ),
        out_shape=shape((2 * count, width + 128), BF16),
        compiler_params=PARAMS,
    )(quarter, expert_ids, gates, grad_out, returned)
    layer_out, gate_grads, token_grads = pl.pallas_call(
        finish_kernel,
        name="finish",
        in_specs=[SMEM] + [VMEM] * 4,
        out_specs=(VMEM,) * 3,
        out_shape=(
            shape((count, model_width), BF16),
            shape((count, chosen), F32),
            shape((count, model_width), BF16),
        ),
        compiler_params=PARAMS,
    )(quarter, packed, moved(packed, 1), moved(packed, 3), moved(packed, 2))
    return layer_out, gate_grads, token_grads, grad_gate, grad_up, grad_down


def solution(mesh):
    rows, cut = P("ep", None), P("ep", "tp", None)
    return jax.shard_map(
        on_device,
        mesh=mesh,
        in_specs=(rows, rows, rows, cut, cut, cut, rows),
        out_specs=(rows, rows, rows, cut, cut, cut),
        check_vma=False,
    )
```

```python
import jax
import jax.numpy as jnp
from jax import lax
from jax.experimental import pallas as pl
from jax.experimental.pallas import tpu as pltpu
from jax.sharding import PartitionSpec as P

SLOTS = 4
BLOCK = 2 * SLOTS
AHEAD_IN = (0, 3, 1, 2)
AHEAD_OUT = (2, 1, 3, 0)
NN = (((1,), (0,)), ((), ()))
NT = (((1,), (1,)), ((), ()))
TN = (((0,), (0,)), ((), ()))
F32 = jnp.float32
BF16 = jnp.bfloat16
ANY = pl.BlockSpec(memory_space=pl.ANY)
VMEM = pl.BlockSpec(memory_space=pltpu.VMEM)
SMEM = pl.BlockSpec(memory_space=pltpu.SMEM)
PARAMS = pltpu.CompilerParams(vmem_limit_bytes=20 * 1024 * 1024)


def dot(left, right, dims=NN):
    return lax.dot_general(left, right, dims, preferred_element_type=F32)


def cost(flops, moved):
    return pl.CostEstimate(flops=flops, bytes_accessed=moved, transcendentals=0)


def row_facts(shape, dim):
    row = lax.broadcasted_iota(jnp.int32, shape, dim)
    second = lax.rem(lax.div(row, SLOTS), 2) == 1
    return lax.div(row, BLOCK), lax.rem(row, SLOTS).astype(F32), second


def dispatch_kernel(quarter, ids_ref, gates_ref, tok_ref, dy_ref, out_ref):
    chosen, count = ids_ref.shape
    shape = (out_ref.shape[0], count)
    expert, slot, second = row_facts(shape, 0)
    named = jnp.zeros(shape, F32)
    gate = jnp.zeros(shape, F32)
    for k in range(chosen):
        hit = ids_ref[k : k + 1, :] == expert
        named = named + jnp.where(hit, 1.0, 0.0)
        gate = gate + jnp.where(hit, gates_ref[k : k + 1, :], 0.0)
    cols = lax.broadcasted_iota(jnp.int32, (count, count), 1)
    earlier = jnp.where(lax.broadcasted_iota(jnp.int32, (count, count), 0) < cols, 1.0, 0.0)
    before = dot(named.astype(BF16), earlier.astype(BF16))
    pick = jnp.where(before == slot, named, 0.0)
    scale = jnp.sum(pick * jnp.where(second, gate, 1.0), axis=1, keepdims=True)
    pick_x = jnp.where(second, 0.0, pick).astype(BF16)
    pick_g = jnp.where(second, pick, 0.0).astype(BF16)
    rows = dot(pick_x, tok_ref[...]) + dot(pick_g, dy_ref[...])
    out_ref[...] = (scale * rows).astype(BF16)


def placing(packed, rows, kind, packed_dim):
    shape = (packed, rows) if packed_dim == 0 else (rows, packed)
    far = lax.broadcasted_iota(jnp.int32, shape, packed_dim)
    near = lax.broadcasted_iota(jnp.int32, shape, 1 - packed_dim)
    place = lax.div(near, SLOTS) * BLOCK + kind * SLOTS + lax.rem(near, SLOTS)
    return jnp.where(far == place, 1.0, 0.0).astype(BF16)


def unpack_kernel(in_ref, x_ref, g_ref):
    for kind, out_ref in enumerate((x_ref, g_ref)):
        pick = placing(in_ref.shape[0], out_ref.shape[0], kind, 1)
        out_ref[...] = dot(pick, in_ref[...]).astype(BF16)


def sum_kernel(own_ref, left_ref, right_ref, out_ref):
    value = own_ref[...].astype(F32) + left_ref[...].astype(F32) + right_ref[...].astype(F32)
    value = value.astype(BF16)
    half = out_ref.shape[1]
    total = None
    for kind in range(2):
        pick = placing(out_ref.shape[0], value.shape[0], kind, 0)
        new = dot(pick, value[:, kind * half : (kind + 1) * half])
        total = new if total is None else total + new
    out_ref[...] = total.astype(BF16)


def columns(q_ref, ahead, width):
    start = lax.rem(q_ref[0] + ahead, 4) * width
    return pl.ds(pl.multiple_of(start, width), width)


def gather_copies(q_ref, pieces, gathered, sems):
    rows, width = pieces[0].shape
    spans = [slice(0, rows)] * 3 + [slice(0, rows // 2), slice(rows // 2, rows)]
    ahead = AHEAD_IN[:3] + (AHEAD_IN[3],) * 2
    return [
        pltpu.make_async_copy(piece, gathered.at[span, columns(q_ref, a, width)], sems.at[n])
        for n, (piece, span, a) in enumerate(zip(pieces, spans, ahead))
    ]


def store_parts(q_ref, outs, width, product):
    for j, ahead in enumerate(AHEAD_OUT):
        part = product(columns(q_ref, ahead, width)).astype(BF16)
        if j == 0:
            half = part.shape[0] // 2
            outs[0][...] = part[:half]
            outs[1][...] = part[half:]
        else:
            outs[j + 1][...] = part


def forward_kernel(q_ref, *refs):
    pieces, (wg_ref, wu_ref, wd_ref), refs = refs[:5], refs[5:8], refs[8:]
    outs, (x_ref, hidden_ref, act_ref, slope_ref, sems) = refs[:5], refs[5:]
    copies = gather_copies(q_ref, pieces, x_ref, sems)
    for copy in copies:
        copy.start()
    for copy in copies:
        copy.wait()
    a = dot(x_ref[...], wg_ref[0], NT)
    b = dot(x_ref[...], wu_ref[0], NT)
    sig = jax.nn.sigmoid(a)
    act = a * sig
    hidden_ref[...] = (act * b).astype(BF16)
    act_ref[...] = act
    slope_ref[...] = b * sig * (1.0 + a * (1.0 - sig))
    store_parts(
        q_ref, outs, pieces[0].shape[1], lambda span: dot(hidden_ref[...], wd_ref[0, :, span])
    )


def backward_kernel(q_ref, *refs):
    pieces, (wg_ref, wu_ref, wd_ref, act_ref, slope_ref), refs = refs[:5], refs[5:10], refs[10:]
    outs, (g_ref, gate_ref, up_ref, sems) = refs[:5], refs[5:]
    copies = gather_copies(q_ref, pieces, g_ref, sems)
    for copy in copies:
        copy.start()
    for copy in copies:
        copy.wait()
    dh = dot(g_ref[...], wd_ref[0], NT)
    gate_ref[...] = (dh * slope_ref[...]).astype(BF16)
    up_ref[...] = (dh * act_ref[...]).astype(BF16)
    store_parts(
        q_ref,
        outs,
        pieces[0].shape[1],
        lambda span: dot(gate_ref[...], wg_ref[0, :, span]) + dot(up_ref[...], wu_ref[0, :, span]),
    )


def weight_kernel(x_ref, g_ref, h_ref, da_ref, du_ref, gate_ref, up_ref, down_ref):
    gate_ref[...] = dot(da_ref[...], x_ref[...], TN).astype(BF16)
    up_ref[...] = dot(du_ref[...], x_ref[...], TN).astype(BF16)
    down_ref[...] = dot(h_ref[...], g_ref[...], TN).astype(BF16)


def picks_by_token(ids_ref, gates_ref, row_count):
    count, chosen = ids_ref.shape
    shape = (count, row_count)
    expert, slot, second = row_facts(shape, 1)
    hits = [ids_ref[:, k : k + 1] == expert for k in range(chosen)]
    named = jnp.zeros(shape, F32)
    gate = jnp.zeros(shape, F32)
    for k in range(chosen):
        named = named + jnp.where(hits[k], 1.0, 0.0)
        gate = gate + jnp.where(hits[k], gates_ref[:, k : k + 1], 0.0)
    rows = lax.broadcasted_iota(jnp.int32, (count, count), 0)
    earlier = jnp.where(lax.broadcasted_iota(jnp.int32, (count, count), 1) < rows, 1.0, 0.0)
    before = dot(earlier.astype(BF16), named.astype(BF16))
    pick = jnp.where(before == slot, named, 0.0)
    return pick, gate, hits, second


def combine_out_kernel(quarter, ids_ref, gates_ref, dy_ref, rows_ref, out_ref):
    count, chosen = ids_ref.shape
    width = dy_ref.shape[1]
    half = width // 2
    rows = rows_ref[...]
    pick, gate, hits, second = picks_by_token(ids_ref, gates_ref, rows.shape[0])
    products = jnp.zeros_like(pick)
    for h in range(2):
        span = slice(h * half, (h + 1) * half)
        mine = jnp.where(second == (h == 1), pick, 0.0)
        weight = mine * gate
        high = weight.astype(BF16)
        low = (weight - high.astype(F32)).astype(BF16)
        out_ref[:, span] = (dot(high, rows) + dot(low, rows)).astype(BF16)
        products = products + mine * dot(dy_ref[:, span], rows, NT)
    lane = lax.broadcasted_iota(jnp.int32, (count, 128), 1)
    share = jnp.zeros((count, 128), F32)
    for k in range(chosen):
        value = jnp.sum(jnp.where(hits[k], products, 0.0), axis=1, keepdims=True)
        share = share + jnp.where(lax.rem(lane, chosen) == k, value, 0.0)
    first = share.astype(BF16).astype(F32)
    rest = share - first
    middle = rest.astype(BF16).astype(F32)
    parts = jnp.where(lane < chosen, first, jnp.where(lane < 2 * chosen, middle, rest - middle))
    out_ref[:, width : width + 128] = parts.astype(BF16)


def combine_back_kernel(ids_ref, gates_ref, rows_ref, out_ref):
    half = rows_ref.shape[1]
    rows = rows_ref[...]
    pick, _, _, second = picks_by_token(ids_ref, gates_ref, rows.shape[0])
    for h in range(2):
        mine = jnp.where(second == (h == 1), pick, 0.0).astype(BF16)
        out_ref[:, h * half : (h + 1) * half] = dot(mine, rows).astype(BF16)


def finish_out_kernel(q_ref, *refs):
    pieces, (layer_ref, gate_ref) = refs[:4], refs[4:]
    count, chosen = gate_ref.shape
    width = layer_ref.shape[1] // 4
    share = jnp.zeros((count, 128), F32)
    for piece, ahead in zip(pieces, AHEAD_IN):
        layer_ref[:, columns(q_ref, ahead, width)] = piece[:, 0:width]
        share = share + piece[:, width : width + 128].astype(F32)
    total = share[:, 0:chosen]
    for j in range(1, 3):
        total = total + share[:, j * chosen : (j + 1) * chosen]
    gate_ref[...] = total


def finish_back_kernel(q_ref, *refs):
    pieces, token_ref = refs[:4], refs[4]
    for piece, ahead in zip(pieces, AHEAD_IN):
        token_ref[:, columns(q_ref, ahead, piece.shape[1])] = piece[...]


def moved(value, ahead):
    return lax.ppermute(value, "tp", [(i, (i + ahead) % 4) for i in range(4)])


def ring_gathered(own):
    half = own.shape[0] // 2
    left, right = moved(own, 1), moved(own, 3)
    far_t, far_b = moved(left[:half], 1), moved(right[half:], 3)
    return own, left, right, far_t, far_b


def added(a, b):
    return (a.astype(F32) + b.astype(F32)).astype(BF16)


def after(value, other):
    return lax.optimization_barrier((value, other))[0]


def ring_terms(partials):
    far_t, far_b, right, left, own = partials
    half = far_t.shape[0]
    in_t, in_b = moved(far_t, 1), moved(far_b, 3)
    from_left = moved(jnp.concatenate([added(right[:half], in_t), right[half:]]), 1)
    from_right = moved(jnp.concatenate([left[:half], added(left[half:], in_b)]), 3)
    return own, from_left, from_right


def swapped(rows, experts):
    block = rows.reshape(experts, BLOCK, rows.shape[-1])
    return lax.all_to_all(block, "ep", 0, 0, tiled=True).reshape(rows.shape)


def on_device(tokens, expert_ids, gates, w_gate, w_up, w_down, grad_out):
    count, model_width = tokens.shape
    chosen = expert_ids.shape[1]
    hidden = w_gate.shape[1]
    experts = lax.axis_size("ep")
    width = model_width // 4
    packed_rows, rows = experts * BLOCK, experts * SLOTS
    quarter = lax.axis_index("tp").astype(jnp.int32).reshape(1)
    shape = jax.ShapeDtypeStruct

    whole = lambda i, q: (0, 0)
    mine = lambda i, q: (0, q[0])
    sent = pl.pallas_call(
        dispatch_kernel,
        name="dispatch",
        grid_spec=pltpu.PrefetchScalarGridSpec(
            num_scalar_prefetch=1,
            grid=(1,),
            in_specs=[
                pl.BlockSpec((chosen, count), whole),
                pl.BlockSpec((chosen, count), whole),
                pl.BlockSpec((count, width), mine),
                pl.BlockSpec((count, width), mine),
            ],
            out_specs=pl.BlockSpec((packed_rows, width), whole),
        ),
        out_shape=shape((packed_rows, width), BF16),
        compiler_params=pltpu.CompilerParams(vmem_limit_bytes=60 * 1024 * 1024),
    )(quarter, expert_ids.T, gates.T, tokens, grad_out)
    piece, part = shape((rows, width), BF16), shape((rows // 2, width), BF16)
    full, narrow, wide = (
        shape((rows, model_width), BF16),
        shape((rows, hidden), BF16),
        shape((rows, hidden), F32),
    )
    x_own, g_own = pl.pallas_call(
        unpack_kernel, name="unpack", out_shape=(piece, piece), compiler_params=PARAMS
    )(swapped(sent, experts))
    x_pieces = ring_gathered(x_own)
    g_pieces = ring_gathered(g_own)

    product = 2 * rows * hidden * model_width

    def expert_call(name, kernel, pieces, extras, kept):
        return pl.pallas_call(
            kernel,
            name=name,
            in_specs=[SMEM] + [ANY] * 5 + [VMEM] * (3 + len(extras)),
            out_specs=(VMEM,) * (6 + len(kept)),
            scratch_shapes=[pltpu.SemaphoreType.DMA((5,))],
            out_shape=(part, part, piece, piece, piece, full) + kept,
            compiler_params=PARAMS,
            cost_estimate=cost(3 * product, 6 * hidden * model_width + 6 * rows * model_width),
        )(quarter, *pieces, w_gate, w_up, w_down, *extras)

    results = expert_call("forward", forward_kernel, x_pieces, (), (narrow, wide, wide))
    y_partials, (x_all, hiddens, act, slope) = results[:5], results[5:]
    y_terms = ring_terms(y_partials)
    results = expert_call("backward", backward_kernel, g_pieces, (act, slope), (narrow, narrow))
    r_partials, (g_all, d_gate, d_up) = results[:5], results[5:]
    r_terms = ring_terms(r_partials)

    def summed(terms):
        return pl.pallas_call(
            sum_kernel,
            name="sum",
            out_shape=shape((packed_rows, width // 2), BF16),
            compiler_params=PARAMS,
        )(*terms)

    y_rows = swapped(summed((after(y_terms[0], r_partials[0]),) + y_terms[1:]), experts)
    r_rows = swapped(summed(r_terms), experts)

    block = pl.BlockSpec((rows, width), lambda i: (0, i))
    side = pl.BlockSpec((rows, hidden), lambda i: (0, 0))
    grad_block = pl.BlockSpec((None, hidden, width), lambda i: (0, 0, i))
    grad_gate, grad_up, grad_down = pl.pallas_call(
        weight_kernel,
        name="weights",
        grid=(4,),
        in_specs=[block, block, side, side, side],
        out_specs=(grad_block,) * 3,
        out_shape=(shape(w_gate.shape, BF16),) * 3,
        compiler_params=PARAMS,
        cost_estimate=cost(3 * product, 2 * model_width * (rows + 3 * hidden)),
    )(x_all, g_all, hiddens, d_gate, d_up)
    r_rows = after(r_rows, grad_down)

    packed = pl.pallas_call(
        combine_out_kernel,
        name="combine_out",
        grid_spec=pltpu.PrefetchScalarGridSpec(
            num_scalar_prefetch=1,
            grid=(1,),
            in_specs=[
                pl.BlockSpec((count, chosen), whole),
                pl.BlockSpec((count, chosen), whole),
                pl.BlockSpec((count, width), mine),
                pl.BlockSpec((packed_rows, width // 2), whole),
            ],
            out_specs=pl.BlockSpec((count, width + 128), whole),
        ),
        out_shape=shape((count, width + 128), BF16),
        compiler_params=PARAMS,
    )(quarter, expert_ids, gates, grad_out, y_rows)
    layer_out, gate_grads = pl.pallas_call(
        finish_out_kernel,
        name="finish_out",
        in_specs=[SMEM] + [VMEM] * 4,
        out_specs=(VMEM,) * 2,
        out_shape=(shape((count, model_width), BF16), shape((count, chosen), F32)),
        compiler_params=PARAMS,
    )(quarter, packed, moved(packed, 1), moved(packed, 3), moved(packed, 2))
    back = pl.pallas_call(
        combine_back_kernel,
        name="combine_back",
        out_shape=shape((count, width), BF16),
        compiler_params=PARAMS,
    )(expert_ids, gates, after(r_rows, layer_out))
    token_grads = pl.pallas_call(
        finish_back_kernel,
        name="finish_back",
        in_specs=[SMEM] + [VMEM] * 4,
        out_specs=VMEM,
        out_shape=shape((count, model_width), BF16),
        compiler_params=PARAMS,
    )(quarter, back, moved(back, 1), moved(back, 3), moved(back, 2))
    return layer_out, gate_grads, token_grads, grad_gate, grad_up, grad_down


def solution(mesh):
    rows, cut = P("ep", None), P("ep", "tp", None)
    return jax.shard_map(
        on_device,
        mesh=mesh,
        in_specs=(rows, rows, rows, cut, cut, cut, rows),
        out_specs=(rows, rows, rows, cut, cut, cut),
        check_vma=False,
    )
```

```python
import jax
import jax.numpy as jnp
from jax import lax
from jax.experimental import pallas as pl
from jax.experimental.pallas import tpu as pltpu
from jax.sharding import PartitionSpec as P

SLOTS = 4
BLOCK = 2 * SLOTS
AHEAD_IN = (0, 3, 1, 2)
AHEAD_OUT = (2, 1, 3, 0)
NN = (((1,), (0,)), ((), ()))
NT = (((1,), (1,)), ((), ()))
TN = (((0,), (0,)), ((), ()))
F32 = jnp.float32
BF16 = jnp.bfloat16
ANY = pl.BlockSpec(memory_space=pl.ANY)
VMEM = pl.BlockSpec(memory_space=pltpu.VMEM)
SMEM = pl.BlockSpec(memory_space=pltpu.SMEM)
PARAMS = pltpu.CompilerParams(vmem_limit_bytes=20 * 1024 * 1024)


def dot(left, right, dims=NN):
    return lax.dot_general(left, right, dims, preferred_element_type=F32)


def cost(flops, moved):
    return pl.CostEstimate(flops=flops, bytes_accessed=moved, transcendentals=0)


def row_facts(shape, dim):
    row = lax.broadcasted_iota(jnp.int32, shape, dim)
    second = lax.rem(lax.div(row, SLOTS), 2) == 1
    return lax.div(row, BLOCK), lax.rem(row, SLOTS).astype(F32), second


def dispatch_kernel(quarter, ids_ref, gates_ref, tok_ref, dy_ref, out_ref):
    chosen, count = ids_ref.shape
    shape = (out_ref.shape[0], count)
    expert, slot, second = row_facts(shape, 0)
    named = jnp.zeros(shape, F32)
    gate = jnp.zeros(shape, F32)
    for k in range(chosen):
        hit = ids_ref[k : k + 1, :] == expert
        named = named + jnp.where(hit, 1.0, 0.0)
        gate = gate + jnp.where(hit, gates_ref[k : k + 1, :], 0.0)
    cols = lax.broadcasted_iota(jnp.int32, (count, count), 1)
    earlier = jnp.where(lax.broadcasted_iota(jnp.int32, (count, count), 0) < cols, 1.0, 0.0)
    before = dot(named.astype(BF16), earlier.astype(BF16))
    pick = jnp.where(before == slot, named, 0.0)
    scale = jnp.sum(pick * jnp.where(second, gate, 1.0), axis=1, keepdims=True)
    pick_x = jnp.where(second, 0.0, pick).astype(BF16)
    pick_g = jnp.where(second, pick, 0.0).astype(BF16)
    rows = dot(pick_x, tok_ref[...]) + dot(pick_g, dy_ref[...])
    out_ref[...] = (scale * rows).astype(BF16)


def placing(packed, rows, kind, packed_dim):
    shape = (packed, rows) if packed_dim == 0 else (rows, packed)
    far = lax.broadcasted_iota(jnp.int32, shape, packed_dim)
    near = lax.broadcasted_iota(jnp.int32, shape, 1 - packed_dim)
    place = lax.div(near, SLOTS) * BLOCK + kind * SLOTS + lax.rem(near, SLOTS)
    return jnp.where(far == place, 1.0, 0.0).astype(BF16)


def unpack_kernel(in_ref, x_ref, g_ref):
    for kind, out_ref in enumerate((x_ref, g_ref)):
        pick = placing(in_ref.shape[0], out_ref.shape[0], kind, 1)
        out_ref[...] = dot(pick, in_ref[...]).astype(BF16)


def columns(q_ref, ahead, width):
    start = lax.rem(q_ref[0] + ahead, 4) * width
    return pl.ds(pl.multiple_of(start, width), width)


def share_kernel(q_ref, wg_ref, wu_ref, wd_ref, right_ref, left_ref, own_ref, sems):
    hidden = wg_ref.shape[1]
    width = own_ref.shape[1]
    half = hidden // 2
    weights = (wg_ref, wu_ref, wd_ref)
    every = slice(0, hidden)
    plan = [(right_ref, n * hidden, n, every, 1) for n in range(3)]
    plan += [(left_ref, n * hidden, n, every, 3) for n in range(3)]
    plan += [(own_ref, n * hidden, n, every, 0) for n in range(3)]
    plan += [(right_ref, 3 * hidden, 0, every, 2), (right_ref, 4 * hidden, 1, slice(0, half), 2)]
    plan += [(left_ref, 3 * hidden, 1, slice(half, hidden), 2)]
    plan += [(left_ref, 3 * hidden + half, 2, every, 2)]
    copies = [
        pltpu.make_async_copy(
            weights[n].at[0, span, columns(q_ref, ahead, width)],
            ref.at[first : first + span.stop - span.start],
            sems.at[m],
        )
        for m, (ref, first, n, span, ahead) in enumerate(plan)
    ]
    for copy in copies:
        copy.start()
    for copy in copies:
        copy.wait()


def inner_kernel(x_ref, g_ref, own_w, left_w, right_w, top_w, bottom_w, top, bottom, right, left, own):
    half = top.shape[0]
    both = 2 * (2 * half // 3)
    x, g = x_ref[...], g_ref[...]
    top[...] = dot(top_w[...], x, NT).astype(BF16)
    bottom[0 : both - half, :] = dot(bottom_w[0 : both - half, :], x, NT).astype(BF16)
    bottom[both - half : half, :] = dot(bottom_w[both - half : half, :], g, NT).astype(BF16)
    for out_ref, w_ref in ((right, right_w), (left, left_w), (own, own_w)):
        out_ref[0:both, :] = dot(w_ref[0:both, :], x, NT).astype(BF16)
        out_ref[both : 2 * half, :] = dot(w_ref[both : 2 * half, :], g, NT).astype(BF16)


def hidden_kernel(own_ref, left_ref, right_ref, out_ref):
    total = own_ref[...].astype(F32) + left_ref[...].astype(F32) + right_ref[...].astype(F32)
    hidden = out_ref.shape[0] // 3
    a, b, dh = (total[n * hidden : (n + 1) * hidden] for n in range(3))
    sig = jax.nn.sigmoid(a)
    act = a * sig
    d_gate = dh * b * sig * (1.0 + a * (1.0 - sig))
    for n, value in enumerate((d_gate, dh * act, act * b)):
        out_ref[n * hidden : (n + 1) * hidden, :] = value.astype(BF16)


def outer_kernel(own, left, right, top, bottom, own_w, left_w, right_w, top_w, bottom_w, out_ref):
    half = top.shape[0]
    both = 2 * (2 * half // 3)
    r_rows = dot(top[...], top_w[...], TN)
    r_rows += dot(bottom[0 : both - half, :], bottom_w[0 : both - half, :], TN)
    y_rows = dot(bottom[both - half : half, :], bottom_w[both - half : half, :], TN)
    for h_ref, w_ref in ((own, own_w), (left, left_w), (right, right_w)):
        r_rows += dot(h_ref[0:both, :], w_ref[0:both, :], TN)
        y_rows += dot(h_ref[both : 2 * half, :], w_ref[both : 2 * half, :], TN)
    total = None
    for kind, value in enumerate((y_rows, r_rows)):
        new = dot(placing(out_ref.shape[0], value.shape[0], kind, 0), value.astype(BF16))
        total = new if total is None else total + new
    out_ref[...] = total.astype(BF16)


def weight_kernel(q_ref, h_ref, *refs):
    x_pieces, g_pieces, outs = refs[:5], refs[5:10], refs[10:]
    hidden = h_ref.shape[0] // 3
    rows, width = x_pieces[0].shape
    for n, (pieces, out_ref) in enumerate(zip((x_pieces, x_pieces, g_pieces), outs)):
        side = h_ref[n * hidden : (n + 1) * hidden, :]
        for j in range(3):
            product = dot(side, pieces[j][...])
            out_ref[0, :, columns(q_ref, AHEAD_IN[j], width)] = product.astype(BF16)
        product = dot(side[:, : rows // 2], pieces[3][...]) + dot(side[:, rows // 2 :], pieces[4][...])
        out_ref[0, :, columns(q_ref, AHEAD_IN[3], width)] = product.astype(BF16)


def combine_kernel(quarter, ids_ref, gates_ref, dy_ref, rows_ref, out_ref):
    count, chosen = ids_ref.shape
    width = dy_ref.shape[1]
    rows = rows_ref[...]
    shape = (count, rows.shape[0])
    expert, slot, second = row_facts(shape, 1)
    hits = [ids_ref[:, k : k + 1] == expert for k in range(chosen)]
    named = jnp.zeros(shape, F32)
    gate = jnp.zeros(shape, F32)
    for k in range(chosen):
        named = named + jnp.where(hits[k], 1.0, 0.0)
        gate = gate + jnp.where(hits[k], gates_ref[:, k : k + 1], 0.0)
    earlier = lax.broadcasted_iota(jnp.int32, (count, count), 1) < lax.broadcasted_iota(
        jnp.int32, (count, count), 0
    )
    before = dot(jnp.where(earlier, 1.0, 0.0).astype(BF16), named.astype(BF16))
    pick = jnp.where(before == slot, named, 0.0)
    pick_y = jnp.where(second, 0.0, pick)
    pick_r = jnp.where(second, pick, 0.0).astype(BF16)
    weight = pick_y * gate
    high = weight.astype(BF16)
    low = (weight - high.astype(F32)).astype(BF16)
    out_ref[0:count, 0:width] = (dot(high, rows) + dot(low, rows)).astype(BF16)
    out_ref[count : 2 * count, 0:width] = dot(pick_r, rows).astype(BF16)
    products = pick_y * dot(dy_ref[...], rows, NT)
    lane = lax.broadcasted_iota(jnp.int32, (count, 128), 1)
    share = jnp.zeros((count, 128), F32)
    for k in range(chosen):
        value = jnp.sum(jnp.where(hits[k], products, 0.0), axis=1, keepdims=True)
        share = share + jnp.where(lax.rem(lane, chosen) == k, value, 0.0)
    first = share.astype(BF16).astype(F32)
    rest = share - first
    middle = rest.astype(BF16).astype(F32)
    parts = jnp.where(lane < chosen, first, jnp.where(lane < 2 * chosen, middle, rest - middle))
    out_ref[0:count, width : width + 128] = parts.astype(BF16)
    out_ref[count : 2 * count, width : width + 128] = jnp.zeros((count, 128), BF16)


def finish_kernel(q_ref, *refs):
    pieces, (layer_ref, gate_ref, token_ref) = refs[:4], refs[4:]
    count, chosen = gate_ref.shape
    width = layer_ref.shape[1] // 4
    share = jnp.zeros((count, 128), F32)
    for j, ahead in enumerate(AHEAD_IN):
        span = columns(q_ref, ahead, width)
        layer_ref[:, span] = pieces[j][0:count, 0:width]
        token_ref[:, span] = pieces[j][count : 2 * count, 0:width]
        share = share + pieces[j][0:count, width : width + 128].astype(F32)
    total = share[:, 0:chosen]
    for j in range(1, 3):
        total = total + share[:, j * chosen : (j + 1) * chosen]
    gate_ref[...] = total


def moved(value, ahead):
    return lax.ppermute(value, "tp", [(i, (i + ahead) % 4) for i in range(4)])


def ring_gathered(own):
    half = own.shape[0] // 2
    left, right = moved(own, 1), moved(own, 3)
    far_t, far_b = moved(left[:half], 1), moved(right[half:], 3)
    return own, left, right, far_t, far_b


def added(a, b):
    return (a.astype(F32) + b.astype(F32)).astype(BF16)


def after(value, other):
    return lax.optimization_barrier((value, other))[0]


def ring_terms(partials):
    far_t, far_b, right, left, own = partials
    half = far_t.shape[0]
    in_t, in_b = moved(far_t, 1), moved(far_b, 3)
    from_left = moved(jnp.concatenate([added(right[:half], in_t), right[half:]]), 1)
    from_right = moved(jnp.concatenate([left[:half], added(left[half:], in_b)]), 3)
    return own, from_left, from_right


def swapped(rows, experts):
    block = rows.reshape(experts, BLOCK, rows.shape[-1])
    return lax.all_to_all(block, "ep", 0, 0, tiled=True).reshape(rows.shape)


def on_device(tokens, expert_ids, gates, w_gate, w_up, w_down, grad_out):
    count, model_width = tokens.shape
    chosen = expert_ids.shape[1]
    hidden = w_gate.shape[1]
    experts = lax.axis_size("ep")
    width = model_width // 4
    packed_rows, rows = experts * BLOCK, experts * SLOTS
    quarter = lax.axis_index("tp").astype(jnp.int32).reshape(1)
    shape = jax.ShapeDtypeStruct

    stacked = 3 * hidden
    sends = shape((stacked * 3 // 2, width), BF16)
    to_right, to_left, own_w = pl.pallas_call(
        share_kernel,
        name="share",
        in_specs=[SMEM] + [ANY] * 3,
        out_specs=(ANY,) * 3,
        scratch_shapes=[pltpu.SemaphoreType.DMA((13,))],
        out_shape=(sends, sends, shape((stacked, width), BF16)),
        compiler_params=PARAMS,
    )(quarter, w_gate, w_up, w_down)
    left_w, right_w = moved(to_right, 1), moved(to_left, 3)
    far_w = moved(left_w[stacked:], 1), moved(right_w[stacked:], 3)
    all_w = (own_w, left_w, right_w) + far_w
    tokens, to_right = lax.optimization_barrier((tokens, to_right))

    whole = lambda i, q: (0, 0)
    mine = lambda i, q: (0, q[0])
    sent = pl.pallas_call(
        dispatch_kernel,
        name="dispatch",
        grid_spec=pltpu.PrefetchScalarGridSpec(
            num_scalar_prefetch=1,
            grid=(1,),
            in_specs=[
                pl.BlockSpec((chosen, count), whole),
                pl.BlockSpec((chosen, count), whole),
                pl.BlockSpec((count, width), mine),
                pl.BlockSpec((count, width), mine),
            ],
            out_specs=pl.BlockSpec((packed_rows, width), whole),
        ),
        out_shape=shape((packed_rows, width), BF16),
        compiler_params=pltpu.CompilerParams(vmem_limit_bytes=60 * 1024 * 1024),
    )(quarter, expert_ids.T, gates.T, tokens, grad_out)
    piece = shape((rows, width), BF16)
    x_own, g_own = pl.pallas_call(
        unpack_kernel, name="unpack", out_shape=(piece, piece), compiler_params=PARAMS
    )(swapped(sent, experts))

    product = 2 * rows * hidden * model_width
    side, part = shape((stacked, rows), BF16), shape((stacked // 2, rows), BF16)
    partials = pl.pallas_call(
        inner_kernel,
        name="inner",
        out_shape=(part, part, side, side, side),
        compiler_params=PARAMS,
        cost_estimate=cost(3 * product, 2 * stacked * model_width),
    )(x_own, g_own, *all_w)
    h_own = pl.pallas_call(
        hidden_kernel, name="hidden", out_shape=side, compiler_params=PARAMS
    )(*ring_terms(partials))
    summed = pl.pallas_call(
        outer_kernel,
        name="outer",
        out_shape=shape((packed_rows, width), BF16),
        compiler_params=PARAMS,
        cost_estimate=cost(3 * product, 2 * stacked * model_width),
    )(*ring_gathered(h_own), *all_w)
    returned = swapped(summed, experts)

    x_pieces = ring_gathered(after(x_own, summed))
    g_pieces = ring_gathered(after(g_own, summed))
    grad_gate, grad_up, grad_down = pl.pallas_call(
        weight_kernel,
        name="weights",
        in_specs=[SMEM] + [VMEM] * 11,
        out_specs=(VMEM,) * 3,
        out_shape=(shape(w_gate.shape, BF16),) * 3,
        compiler_params=PARAMS,
        cost_estimate=cost(3 * product, 2 * model_width * (rows + 3 * hidden)),
    )(quarter, h_own, *x_pieces, *g_pieces)

    packed = pl.pallas_call(
        combine_kernel,
        name="combine",
        grid_spec=pltpu.PrefetchScalarGridSpec(
            num_scalar_prefetch=1,
            grid=(1,),
            in_specs=[
                pl.BlockSpec((count, chosen), whole),
                pl.BlockSpec((count, chosen), whole),
                pl.BlockSpec((count, width), mine),
                pl.BlockSpec((packed_rows, width), whole),
            ],
            out_specs=pl.BlockSpec((2 * count, width + 128), whole),
        ),
        out_shape=shape((2 * count, width + 128), BF16),
        compiler_params=PARAMS,
    )(quarter, expert_ids, gates, grad_out, returned)
    layer_out, gate_grads, token_grads = pl.pallas_call(
        finish_kernel,
        name="finish",
        in_specs=[SMEM] + [VMEM] * 4,
        out_specs=(VMEM,) * 3,
        out_shape=(
            shape((count, model_width), BF16),
            shape((count, chosen), F32),
            shape((count, model_width), BF16),
        ),
        compiler_params=PARAMS,
    )(quarter, packed, moved(packed, 1), moved(packed, 3), moved(packed, 2))
    return layer_out, gate_grads, token_grads, grad_gate, grad_up, grad_down


def solution(mesh):
    rows, cut = P("ep", None), P("ep", "tp", None)
    return jax.shard_map(
        on_device,
        mesh=mesh,
        in_specs=(rows, rows, rows, cut, cut, cut, rows),
        out_specs=(rows, rows, rows, cut, cut, cut),
        check_vma=False,
    )
```

```python
import jax
import jax.numpy as jnp
from jax import lax
from jax.experimental import pallas as pl
from jax.experimental.pallas import tpu as pltpu
from jax.sharding import PartitionSpec as P

SLOTS = 4
BLOCK = 2 * SLOTS
AHEAD_IN = (0, 3, 1, 2)
AHEAD_OUT = (2, 1, 3, 0)
NN = (((1,), (0,)), ((), ()))
NT = (((1,), (1,)), ((), ()))
TN = (((0,), (0,)), ((), ()))
F32 = jnp.float32
BF16 = jnp.bfloat16
ANY = pl.BlockSpec(memory_space=pl.ANY)
VMEM = pl.BlockSpec(memory_space=pltpu.VMEM)
SMEM = pl.BlockSpec(memory_space=pltpu.SMEM)
PARAMS = pltpu.CompilerParams(vmem_limit_bytes=20 * 1024 * 1024)


def dot(left, right, dims=NN):
    return lax.dot_general(left, right, dims, preferred_element_type=F32)


def cost(flops, moved):
    return pl.CostEstimate(flops=flops, bytes_accessed=moved, transcendentals=0)


def row_facts(shape, dim):
    row = lax.broadcasted_iota(jnp.int32, shape, dim)
    second = lax.rem(lax.div(row, SLOTS), 2) == 1
    return lax.div(row, BLOCK), lax.rem(row, SLOTS).astype(F32), second


def dispatch_kernel(quarter, ids_ref, gates_ref, tok_ref, dy_ref, out_ref):
    chosen, count = ids_ref.shape
    shape = (out_ref.shape[0], count)
    expert, slot, second = row_facts(shape, 0)
    named = jnp.zeros(shape, F32)
    gate = jnp.zeros(shape, F32)
    for k in range(chosen):
        hit = ids_ref[k : k + 1, :] == expert
        named = named + jnp.where(hit, 1.0, 0.0)
        gate = gate + jnp.where(hit, gates_ref[k : k + 1, :], 0.0)
    cols = lax.broadcasted_iota(jnp.int32, (count, count), 1)
    earlier = jnp.where(lax.broadcasted_iota(jnp.int32, (count, count), 0) < cols, 1.0, 0.0)
    before = dot(named.astype(BF16), earlier.astype(BF16))
    pick = jnp.where(before == slot, named, 0.0)
    scale = jnp.sum(pick * jnp.where(second, gate, 1.0), axis=1, keepdims=True)
    pick_x = jnp.where(second, 0.0, pick).astype(BF16)
    pick_g = jnp.where(second, pick, 0.0).astype(BF16)
    rows = dot(pick_x, tok_ref[...]) + dot(pick_g, dy_ref[...])
    out_ref[...] = (scale * rows).astype(BF16)


def placing(packed, rows, kind, packed_dim):
    shape = (packed, rows) if packed_dim == 0 else (rows, packed)
    far = lax.broadcasted_iota(jnp.int32, shape, packed_dim)
    near = lax.broadcasted_iota(jnp.int32, shape, 1 - packed_dim)
    place = lax.div(near, SLOTS) * BLOCK + kind * SLOTS + lax.rem(near, SLOTS)
    return jnp.where(far == place, 1.0, 0.0).astype(BF16)


def unpack_kernel(in_ref, out_ref):
    rows = out_ref.shape[0] // 2
    for kind in range(2):
        pick = placing(in_ref.shape[0], rows, kind, 1)
        out_ref[kind * rows : (kind + 1) * rows, :] = dot(pick, in_ref[...]).astype(BF16)


def columns(q_ref, ahead, width):
    start = lax.rem(q_ref[0] + ahead, 4) * width
    return pl.ds(pl.multiple_of(start, width), width)


def share_kernel(q_ref, wg_ref, wu_ref, wd_ref, right_ref, left_ref, own_ref, sems):
    hidden = wg_ref.shape[1]
    width = own_ref.shape[1]
    half = hidden // 2
    weights = (wg_ref, wu_ref, wd_ref)
    every = slice(0, hidden)
    plan = [(right_ref, n * hidden, n, every, 1) for n in range(3)]
    plan += [(left_ref, n * hidden, n, every, 3) for n in range(3)]
    plan += [(own_ref, n * hidden, n, every, 0) for n in range(3)]
    plan += [(right_ref, 3 * hidden, 0, every, 2), (right_ref, 4 * hidden, 1, slice(0, half), 2)]
    plan += [(left_ref, 3 * hidden, 1, slice(half, hidden), 2)]
    plan += [(left_ref, 3 * hidden + half, 2, every, 2)]
    copies = [
        pltpu.make_async_copy(
            weights[n].at[0, span, columns(q_ref, ahead, width)],
            ref.at[first : first + span.stop - span.start],
            sems.at[m],
        )
        for m, (ref, first, n, span, ahead) in enumerate(plan)
    ]
    for copy in copies:
        copy.start()
    for copy in copies:
        copy.wait()


def inner_kernel(rows_ref, own_w, left_w, right_w, top_w, bottom_w, top, bottom, right, left, own):
    half = top.shape[0]
    both = 2 * (2 * half // 3)
    count = rows_ref.shape[0] // 2
    x, g = rows_ref[0:count, :], rows_ref[count : 2 * count, :]
    top[...] = dot(top_w[...], x, NT).astype(BF16)
    bottom[0 : both - half, :] = dot(bottom_w[0 : both - half, :], x, NT).astype(BF16)
    bottom[both - half : half, :] = dot(bottom_w[both - half : half, :], g, NT).astype(BF16)
    for out_ref, w_ref in ((right, right_w), (left, left_w), (own, own_w)):
        out_ref[0:both, :] = dot(w_ref[0:both, :], x, NT).astype(BF16)
        out_ref[both : 2 * half, :] = dot(w_ref[both : 2 * half, :], g, NT).astype(BF16)


def hidden_kernel(own_ref, left_ref, right_ref, out_ref):
    total = own_ref[...].astype(F32) + left_ref[...].astype(F32) + right_ref[...].astype(F32)
    hidden = out_ref.shape[0] // 3
    a, b, dh = (total[n * hidden : (n + 1) * hidden] for n in range(3))
    sig = jax.nn.sigmoid(a)
    act = a * sig
    d_gate = dh * b * sig * (1.0 + a * (1.0 - sig))
    for n, value in enumerate((d_gate, dh * act, act * b)):
        out_ref[n * hidden : (n + 1) * hidden, :] = value.astype(BF16)


def outer_kernel(own, left, right, top, bottom, own_w, left_w, right_w, top_w, bottom_w, out_ref):
    half = top.shape[0]
    both = 2 * (2 * half // 3)
    r_rows = dot(top[...], top_w[...], TN)
    r_rows += dot(bottom[0 : both - half, :], bottom_w[0 : both - half, :], TN)
    y_rows = dot(bottom[both - half : half, :], bottom_w[both - half : half, :], TN)
    for h_ref, w_ref in ((own, own_w), (left, left_w), (right, right_w)):
        r_rows += dot(h_ref[0:both, :], w_ref[0:both, :], TN)
        y_rows += dot(h_ref[both : 2 * half, :], w_ref[both : 2 * half, :], TN)
    total = None
    for kind, value in enumerate((y_rows, r_rows)):
        new = dot(placing(out_ref.shape[0], value.shape[0], kind, 0), value.astype(BF16))
        total = new if total is None else total + new
    out_ref[...] = total.astype(BF16)


def weight_kernel(q_ref, h_ref, own, left, right, far_x, far_g, *outs):
    hidden = h_ref.shape[0] // 3
    rows, width = far_x.shape
    for n, out_ref in enumerate(outs):
        side = h_ref[n * hidden : (n + 1) * hidden, :]
        span, far = (slice(0, rows), far_x) if n < 2 else (slice(rows, 2 * rows), far_g)
        pieces = (own[span, :], left[span, :], right[span, :], far[...])
        for piece, ahead in zip(pieces, AHEAD_IN):
            out_ref[0, :, columns(q_ref, ahead, width)] = dot(side, piece).astype(BF16)


def combine_kernel(quarter, ids_ref, gates_ref, dy_ref, rows_ref, out_ref):
    count, chosen = ids_ref.shape
    width = dy_ref.shape[1]
    rows = rows_ref[...]
    shape = (count, rows.shape[0])
    expert, slot, second = row_facts(shape, 1)
    hits = [ids_ref[:, k : k + 1] == expert for k in range(chosen)]
    named = jnp.zeros(shape, F32)
    gate = jnp.zeros(shape, F32)
    for k in range(chosen):
        named = named + jnp.where(hits[k], 1.0, 0.0)
        gate = gate + jnp.where(hits[k], gates_ref[:, k : k + 1], 0.0)
    earlier = lax.broadcasted_iota(jnp.int32, (count, count), 1) < lax.broadcasted_iota(
        jnp.int32, (count, count), 0
    )
    before = dot(jnp.where(earlier, 1.0, 0.0).astype(BF16), named.astype(BF16))
    pick = jnp.where(before == slot, named, 0.0)
    pick_y = jnp.where(second, 0.0, pick)
    pick_r = jnp.where(second, pick, 0.0).astype(BF16)
    weight = pick_y * gate
    high = weight.astype(BF16)
    low = (weight - high.astype(F32)).astype(BF16)
    out_ref[0:count, 0:width] = (dot(high, rows) + dot(low, rows)).astype(BF16)
    out_ref[count : 2 * count, 0:width] = dot(pick_r, rows).astype(BF16)
    products = pick_y * dot(dy_ref[...], rows, NT)
    lane = lax.broadcasted_iota(jnp.int32, (count, 128), 1)
    share = jnp.zeros((count, 128), F32)
    for k in range(chosen):
        value = jnp.sum(jnp.where(hits[k], products, 0.0), axis=1, keepdims=True)
        share = share + jnp.where(lax.rem(lane, chosen) == k, value, 0.0)
    first = share.astype(BF16).astype(F32)
    rest = share - first
    middle = rest.astype(BF16).astype(F32)
    parts = jnp.where(lane < chosen, first, jnp.where(lane < 2 * chosen, middle, rest - middle))
    out_ref[0:count, width : width + 128] = parts.astype(BF16)
    out_ref[count : 2 * count, width : width + 128] = jnp.zeros((count, 128), BF16)


def finish_kernel(q_ref, *refs):
    pieces, (layer_ref, gate_ref, token_ref) = refs[:4], refs[4:]
    count, chosen = gate_ref.shape
    width = layer_ref.shape[1] // 4
    share = jnp.zeros((count, 128), F32)
    for j, ahead in enumerate(AHEAD_IN):
        span = columns(q_ref, ahead, width)
        layer_ref[:, span] = pieces[j][0:count, 0:width]
        token_ref[:, span] = pieces[j][count : 2 * count, 0:width]
        share = share + pieces[j][0:count, width : width + 128].astype(F32)
    total = share[:, 0:chosen]
    for j in range(1, 3):
        total = total + share[:, j * chosen : (j + 1) * chosen]
    gate_ref[...] = total


def moved(value, ahead):
    return lax.ppermute(value, "tp", [(i, (i + ahead) % 4) for i in range(4)])


def ring_gathered(own):
    half = own.shape[0] // 2
    left, right = moved(own, 1), moved(own, 3)
    far_t, far_b = moved(left[:half], 1), moved(right[half:], 3)
    return own, left, right, far_t, far_b


def added(a, b):
    return (a.astype(F32) + b.astype(F32)).astype(BF16)


def after(value, other):
    return lax.optimization_barrier((value, other))[0]


def ring_terms(partials):
    far_t, far_b, right, left, own = partials
    half = far_t.shape[0]
    in_t, in_b = moved(far_t, 1), moved(far_b, 3)
    from_left = moved(jnp.concatenate([added(right[:half], in_t), right[half:]]), 1)
    from_right = moved(jnp.concatenate([left[:half], added(left[half:], in_b)]), 3)
    return own, from_left, from_right


def swapped(rows, experts):
    block = rows.reshape(experts, BLOCK, rows.shape[-1])
    return lax.all_to_all(block, "ep", 0, 0, tiled=True).reshape(rows.shape)


def on_device(tokens, expert_ids, gates, w_gate, w_up, w_down, grad_out):
    count, model_width = tokens.shape
    chosen = expert_ids.shape[1]
    hidden = w_gate.shape[1]
    experts = lax.axis_size("ep")
    width = model_width // 4
    packed_rows, rows = experts * BLOCK, experts * SLOTS
    quarter = lax.axis_index("tp").astype(jnp.int32).reshape(1)
    shape = jax.ShapeDtypeStruct

    stacked = 3 * hidden
    sends = shape((stacked * 3 // 2, width), BF16)
    to_right, to_left, own_w = pl.pallas_call(
        share_kernel,
        name="share",
        in_specs=[SMEM] + [ANY] * 3,
        out_specs=(ANY,) * 3,
        scratch_shapes=[pltpu.SemaphoreType.DMA((13,))],
        out_shape=(sends, sends, shape((stacked, width), BF16)),
        compiler_params=pltpu.CompilerParams(vmem_limit_bytes=60 * 1024 * 1024),
    )(quarter, w_gate, w_up, w_down)
    left_w, right_w = moved(to_right, 1), moved(to_left, 3)
    far_w = moved(left_w[stacked:], 1), moved(right_w[stacked:], 3)
    all_w = (own_w, left_w, right_w) + far_w
    tokens, to_right = lax.optimization_barrier((tokens, to_right))

    whole = lambda i, q: (0, 0)
    mine = lambda i, q: (0, q[0])
    sent = pl.pallas_call(
        dispatch_kernel,
        name="dispatch",
        grid_spec=pltpu.PrefetchScalarGridSpec(
            num_scalar_prefetch=1,
            grid=(1,),
            in_specs=[
                pl.BlockSpec((chosen, count), whole),
                pl.BlockSpec((chosen, count), whole),
                pl.BlockSpec((count, width), mine),
                pl.BlockSpec((count, width), mine),
            ],
            out_specs=pl.BlockSpec((packed_rows, width), whole),
        ),
        out_shape=shape((packed_rows, width), BF16),
        compiler_params=pltpu.CompilerParams(vmem_limit_bytes=60 * 1024 * 1024),
    )(quarter, expert_ids.T, gates.T, tokens, grad_out)
    own_rows = pl.pallas_call(
        unpack_kernel,
        name="unpack",
        out_shape=shape((packed_rows, width), BF16),
        compiler_params=PARAMS,
    )(swapped(sent, experts))

    product = 2 * rows * hidden * model_width
    side, part = shape((stacked, rows), BF16), shape((stacked // 2, rows), BF16)
    partials = pl.pallas_call(
        inner_kernel,
        name="inner",
        out_shape=(part, part, side, side, side),
        compiler_params=PARAMS,
        cost_estimate=cost(3 * product, 2 * stacked * model_width),
    )(own_rows, *all_w)
    h_own = pl.pallas_call(
        hidden_kernel, name="hidden", out_shape=side, compiler_params=PARAMS
    )(*ring_terms(partials))
    h_pieces = ring_gathered(h_own)
    summed = pl.pallas_call(
        outer_kernel,
        name="outer",
        out_shape=shape((packed_rows, width), BF16),
        compiler_params=PARAMS,
        cost_estimate=cost(3 * product, 2 * stacked * model_width),
    )(*h_pieces, *all_w)
    returned = swapped(summed, experts)

    pieces = ring_gathered(after(own_rows, h_pieces[3]))
    grad_gate, grad_up, grad_down = pl.pallas_call(
        weight_kernel,
        name="weights",
        in_specs=[SMEM] + [VMEM] * 6,
        out_specs=(VMEM,) * 3,
        out_shape=(shape(w_gate.shape, BF16),) * 3,
        compiler_params=PARAMS,
        cost_estimate=cost(3 * product, 2 * model_width * (rows + 3 * hidden)),
    )(quarter, h_own, *pieces)

    packed = pl.pallas_call(
        combine_kernel,
        name="combine",
        grid_spec=pltpu.PrefetchScalarGridSpec(
            num_scalar_prefetch=1,
            grid=(1,),
            in_specs=[
                pl.BlockSpec((count, chosen), whole),
                pl.BlockSpec((count, chosen), whole),
                pl.BlockSpec((count, width), mine),
                pl.BlockSpec((packed_rows, width), whole),
            ],
            out_specs=pl.BlockSpec((2 * count, width + 128), whole),
        ),
        out_shape=shape((2 * count, width + 128), BF16),
        compiler_params=PARAMS,
    )(quarter, expert_ids, gates, grad_out, returned)
    layer_out, gate_grads, token_grads = pl.pallas_call(
        finish_kernel,
        name="finish",
        in_specs=[SMEM] + [VMEM] * 4,
        out_specs=(VMEM,) * 3,
        out_shape=(
            shape((count, model_width), BF16),
            shape((count, chosen), F32),
            shape((count, model_width), BF16),
        ),
        compiler_params=PARAMS,
    )(quarter, packed, moved(packed, 1), moved(packed, 3), moved(packed, 2))
    return layer_out, gate_grads, token_grads, grad_gate, grad_up, grad_down


def solution(mesh):
    rows, cut = P("ep", None), P("ep", "tp", None)
    return jax.shard_map(
        on_device,
        mesh=mesh,
        in_specs=(rows, rows, rows, cut, cut, cut, rows),
        out_specs=(rows, rows, rows, cut, cut, cut),
        check_vma=False,
    )
```

```python
import functools

import jax
import jax.numpy as jnp
from jax import lax
from jax.experimental import pallas as pl
from jax.experimental.pallas import tpu as pltpu
from jax.sharding import PartitionSpec as P

SLOTS = 4
BLOCK = 2 * SLOTS
AHEAD_IN = (0, 3, 1, 2)
AHEAD_OUT = (2, 1, 3, 0)
NN = (((1,), (0,)), ((), ()))
NT = (((1,), (1,)), ((), ()))
TN = (((0,), (0,)), ((), ()))
F32 = jnp.float32
BF16 = jnp.bfloat16
ANY = pl.BlockSpec(memory_space=pl.ANY)
VMEM = pl.BlockSpec(memory_space=pltpu.VMEM)
SMEM = pl.BlockSpec(memory_space=pltpu.SMEM)
PARAMS = pltpu.CompilerParams(vmem_limit_bytes=20 * 1024 * 1024)


def dot(left, right, dims=NN):
    return lax.dot_general(left, right, dims, preferred_element_type=F32)


def cost(flops, moved):
    return pl.CostEstimate(flops=flops, bytes_accessed=moved, transcendentals=0)


def row_facts(shape, dim):
    row = lax.broadcasted_iota(jnp.int32, shape, dim)
    second = lax.rem(lax.div(row, SLOTS), 2) == 1
    return lax.div(row, BLOCK), lax.rem(row, SLOTS).astype(F32), second


def dispatch_kernel(quarter, ids_ref, gates_ref, tok_ref, dy_ref, out_ref):
    chosen, count = ids_ref.shape
    shape = (out_ref.shape[0], count)
    expert, slot, second = row_facts(shape, 0)
    named = jnp.zeros(shape, F32)
    gate = jnp.zeros(shape, F32)
    for k in range(chosen):
        hit = ids_ref[k : k + 1, :] == expert
        named = named + jnp.where(hit, 1.0, 0.0)
        gate = gate + jnp.where(hit, gates_ref[k : k + 1, :], 0.0)
    cols = lax.broadcasted_iota(jnp.int32, (count, count), 1)
    earlier = jnp.where(lax.broadcasted_iota(jnp.int32, (count, count), 0) < cols, 1.0, 0.0)
    before = dot(named.astype(BF16), earlier.astype(BF16))
    pick = jnp.where(before == slot, named, 0.0)
    scale = jnp.sum(pick * jnp.where(second, gate, 1.0), axis=1, keepdims=True)
    pick_x = jnp.where(second, 0.0, pick).astype(BF16)
    pick_g = jnp.where(second, pick, 0.0).astype(BF16)
    rows = dot(pick_x, tok_ref[...]) + dot(pick_g, dy_ref[...])
    out_ref[...] = (scale * rows).astype(BF16)


def placing(packed, rows, kind, packed_dim):
    shape = (packed, rows) if packed_dim == 0 else (rows, packed)
    far = lax.broadcasted_iota(jnp.int32, shape, packed_dim)
    near = lax.broadcasted_iota(jnp.int32, shape, 1 - packed_dim)
    place = lax.div(near, SLOTS) * BLOCK + kind * SLOTS + lax.rem(near, SLOTS)
    return jnp.where(far == place, 1.0, 0.0).astype(BF16)


def unpack_kernel(in_ref, x_ref, g_ref):
    for kind, out_ref in enumerate((x_ref, g_ref)):
        pick = placing(in_ref.shape[0], out_ref.shape[0], kind, 1)
        out_ref[...] = dot(pick, in_ref[...]).astype(BF16)


def columns(q_ref, ahead, width):
    start = lax.rem(q_ref[0] + ahead, 4) * width
    return pl.ds(pl.multiple_of(start, width), width)


def share_kernel(q_ref, wg_ref, wu_ref, wd_ref, to_right, to_left, own, sems):
    hidden = wg_ref.shape[1]
    width = own.shape[1]
    half = hidden // 2
    weights = (wg_ref, wu_ref, wd_ref)
    every, low, high = slice(0, hidden), slice(0, half), slice(half, hidden)

    def upper(ref, first, ahead):
        return [(ref, first, 0, every, ahead), (ref, first + hidden, 1, low, ahead)]

    def lower(ref, first, ahead):
        return [(ref, first, 1, high, ahead), (ref, first + half, 2, every, ahead)]

    middle = hidden + half
    plan = upper(to_right, 0, 2) + lower(to_left, 0, 2)
    for ref, first, ahead in ((to_right, middle, 1), (to_left, middle, 3), (own, 0, 0)):
        plan += upper(ref, first, ahead) + lower(ref, first + middle, ahead)
    copies = [
        pltpu.make_async_copy(
            weights[n].at[0, span, columns(q_ref, ahead, width)],
            ref.at[first : first + span.stop - span.start],
            sems.at[m],
        )
        for m, (ref, first, n, span, ahead) in enumerate(plan)
    ]
    for copy in copies:
        copy.start()
    for copy in copies:
        copy.wait()


def weight_parts(own, left, right, top, bottom):
    half = top.shape[0]
    return (
        (top, bottom),
        (right.at[half : 2 * half], right.at[2 * half : 3 * half]),
        (left.at[half : 2 * half], left.at[2 * half : 3 * half]),
        (own.at[0:half], own.at[half : 2 * half]),
    )


def inner_kernel(x_ref, g_ref, *refs):
    weights, (far_t, far_b, right, left, own) = weight_parts(*refs[:5]), refs[5:]
    half = far_t.shape[0]
    cut = half // 3
    outs = [(far_t, far_b)]
    outs += [(ref.at[0:half], ref.at[half : 2 * half]) for ref in (right, left, own)]
    x, g = x_ref[...], g_ref[...]
    for (upper, lower), (upper_out, lower_out) in zip(weights, outs):
        upper_out[...] = dot(upper[...], x, NT).astype(BF16)
        lower_out[0:cut, :] = dot(lower[0:cut, :], x, NT).astype(BF16)
        lower_out[cut:half, :] = dot(lower[cut:half, :], g, NT).astype(BF16)


def hidden_kernel(own_ref, left_ref, right_ref, out_ref):
    total = own_ref[...].astype(F32) + left_ref[...].astype(F32) + right_ref[...].astype(F32)
    hidden = out_ref.shape[0] // 3
    a, b, dh = (total[n * hidden : (n + 1) * hidden] for n in range(3))
    sig = jax.nn.sigmoid(a)
    act = a * sig
    d_gate = dh * b * sig * (1.0 + a * (1.0 - sig))
    for n, value in enumerate((d_gate, dh * act, act * b)):
        out_ref[n * hidden : (n + 1) * hidden, :] = value.astype(BF16)


def outer_kernel(own, left, right, far_t, far_b, *refs):
    weights, out_ref = weight_parts(*refs[:5]), refs[5]
    half = far_t.shape[0]
    cut = half // 3
    sides = [(far_t, far_b)]
    sides += [(ref.at[0:half], ref.at[half : 2 * half]) for ref in (right, left, own)]
    r_rows, y_rows = None, None
    for (upper, lower), (upper_h, lower_h) in zip(weights, sides):
        new = dot(upper_h[...], upper[...], TN) + dot(lower_h[0:cut, :], lower[0:cut, :], TN)
        r_rows = new if r_rows is None else r_rows + new
        new = dot(lower_h[cut:half, :], lower[cut:half, :], TN)
        y_rows = new if y_rows is None else y_rows + new
    total = None
    for kind, value in enumerate((y_rows, r_rows)):
        new = dot(placing(out_ref.shape[0], value.shape[0], kind, 0), value.astype(BF16))
        total = new if total is None else total + new
    out_ref[...] = total.astype(BF16)


def weight_kernel(first, q_ref, h_ref, own, left, right, far_t, far_b, *outs):
    hidden = h_ref.shape[0] // 3
    rows, width = own.shape
    half = rows // 2
    for n, out_ref in enumerate(outs):
        side = h_ref[(first + n) * hidden : (first + n + 1) * hidden, :]
        for piece, ahead in zip((own, left, right), AHEAD_IN):
            out_ref[0, :, columns(q_ref, ahead, width)] = dot(side, piece[...]).astype(BF16)
        far = dot(side[:, :half], far_t[...]) + dot(side[:, half:], far_b[...])
        out_ref[0, :, columns(q_ref, AHEAD_IN[3], width)] = far.astype(BF16)


def combine_kernel(quarter, ids_ref, gates_ref, dy_ref, rows_ref, out_ref):
    count, chosen = ids_ref.shape
    width = dy_ref.shape[1]
    rows = rows_ref[...]
    shape = (count, rows.shape[0])
    expert, slot, second = row_facts(shape, 1)
    hits = [ids_ref[:, k : k + 1] == expert for k in range(chosen)]
    named = jnp.zeros(shape, F32)
    gate = jnp.zeros(shape, F32)
    for k in range(chosen):
        named = named + jnp.where(hits[k], 1.0, 0.0)
        gate = gate + jnp.where(hits[k], gates_ref[:, k : k + 1], 0.0)
    earlier = lax.broadcasted_iota(jnp.int32, (count, count), 1) < lax.broadcasted_iota(
        jnp.int32, (count, count), 0
    )
    before = dot(jnp.where(earlier, 1.0, 0.0).astype(BF16), named.astype(BF16))
    pick = jnp.where(before == slot, named, 0.0)
    pick_y = jnp.where(second, 0.0, pick)
    pick_r = jnp.where(second, pick, 0.0).astype(BF16)
    weight = pick_y * gate
    high = weight.astype(BF16)
    low = (weight - high.astype(F32)).astype(BF16)
    out_ref[0:count, 0:width] = (dot(high, rows) + dot(low, rows)).astype(BF16)
    out_ref[count : 2 * count, 0:width] = dot(pick_r, rows).astype(BF16)
    products = pick_y * dot(dy_ref[...], rows, NT)
    lane = lax.broadcasted_iota(jnp.int32, (count, 128), 1)
    share = jnp.zeros((count, 128), F32)
    for k in range(chosen):
        value = jnp.sum(jnp.where(hits[k], products, 0.0), axis=1, keepdims=True)
        share = share + jnp.where(lax.rem(lane, chosen) == k, value, 0.0)
    first = share.astype(BF16).astype(F32)
    rest = share - first
    middle = rest.astype(BF16).astype(F32)
    parts = jnp.where(lane < chosen, first, jnp.where(lane < 2 * chosen, middle, rest - middle))
    out_ref[0:count, width : width + 128] = parts.astype(BF16)
    out_ref[count : 2 * count, width : width + 128] = jnp.zeros((count, 128), BF16)


def finish_kernel(q_ref, *refs):
    pieces, (layer_ref, gate_ref, token_ref) = refs[:4], refs[4:]
    count, chosen = gate_ref.shape
    width = layer_ref.shape[1] // 4
    share = jnp.zeros((count, 128), F32)
    for j, ahead in enumerate(AHEAD_IN):
        span = columns(q_ref, ahead, width)
        layer_ref[:, span] = pieces[j][0:count, 0:width]
        token_ref[:, span] = pieces[j][count : 2 * count, 0:width]
        share = share + pieces[j][0:count, width : width + 128].astype(F32)
    total = share[:, 0:chosen]
    for j in range(1, 3):
        total = total + share[:, j * chosen : (j + 1) * chosen]
    gate_ref[...] = total


def moved(value, ahead):
    return lax.ppermute(value, "tp", [(i, (i + ahead) % 4) for i in range(4)])


def ring_gathered(own):
    half = own.shape[0] // 2
    left, right = moved(own, 1), moved(own, 3)
    far_t, far_b = moved(left[:half], 1), moved(right[half:], 3)
    return own, left, right, far_t, far_b


def added(a, b):
    return (a.astype(F32) + b.astype(F32)).astype(BF16)


def after(value, other):
    return lax.optimization_barrier((value, other))[0]


def ring_terms(partials):
    far_t, far_b, right, left, own = partials
    half = far_t.shape[0]
    in_t, in_b = moved(far_t, 1), moved(far_b, 3)
    from_left = moved(jnp.concatenate([added(right[:half], in_t), right[half:]]), 1)
    from_right = moved(jnp.concatenate([left[:half], added(left[half:], in_b)]), 3)
    return own, from_left, from_right


def swapped(rows, experts):
    block = rows.reshape(experts, BLOCK, rows.shape[-1])
    return lax.all_to_all(block, "ep", 0, 0, tiled=True).reshape(rows.shape)


def on_device(tokens, expert_ids, gates, w_gate, w_up, w_down, grad_out):
    count, model_width = tokens.shape
    chosen = expert_ids.shape[1]
    hidden = w_gate.shape[1]
    experts = lax.axis_size("ep")
    width = model_width // 4
    packed_rows, rows = experts * BLOCK, experts * SLOTS
    quarter = lax.axis_index("tp").astype(jnp.int32).reshape(1)
    shape = jax.ShapeDtypeStruct

    stacked = 3 * hidden
    sends = shape((stacked * 3 // 2, width), BF16)
    to_right, to_left, own_w = pl.pallas_call(
        share_kernel,
        name="share",
        in_specs=[SMEM] + [ANY] * 3,
        out_specs=(VMEM,) * 3,
        scratch_shapes=[pltpu.SemaphoreType.DMA((16,))],
        out_shape=(sends, sends, shape((stacked, width), BF16)),
        compiler_params=pltpu.CompilerParams(vmem_limit_bytes=60 * 1024 * 1024),
    )(quarter, w_gate, w_up, w_down)
    left_w, right_w = moved(to_right, 1), moved(to_left, 3)
    far_w = moved(left_w[: stacked // 2], 1), moved(right_w[: stacked // 2], 3)
    all_w = (own_w, left_w, right_w) + far_w
    tokens = after(tokens, to_right)

    whole = lambda i, q: (0, 0)
    mine = lambda i, q: (0, q[0])
    sent = pl.pallas_call(
        dispatch_kernel,
        name="dispatch",
        grid_spec=pltpu.PrefetchScalarGridSpec(
            num_scalar_prefetch=1,
            grid=(1,),
            in_specs=[
                pl.BlockSpec((chosen, count), whole),
                pl.BlockSpec((chosen, count), whole),
                pl.BlockSpec((count, width), mine),
                pl.BlockSpec((count, width), mine),
            ],
            out_specs=pl.BlockSpec((packed_rows, width), whole),
        ),
        out_shape=shape((packed_rows, width), BF16),
        compiler_params=pltpu.CompilerParams(vmem_limit_bytes=60 * 1024 * 1024),
    )(quarter, expert_ids.T, gates.T, tokens, grad_out)
    piece = shape((rows, width), BF16)
    x_own, g_own = pl.pallas_call(
        unpack_kernel, name="unpack", out_shape=(piece, piece), compiler_params=PARAMS
    )(swapped(sent, experts))

    product = 2 * rows * hidden * model_width
    side, part = shape((stacked, rows), BF16), shape((stacked // 2, rows), BF16)
    partials = pl.pallas_call(
        inner_kernel,
        name="inner",
        out_shape=(part, part, side, side, side),
        compiler_params=PARAMS,
        cost_estimate=cost(3 * product, 2 * stacked * model_width),
    )(x_own, g_own, *all_w)
    h_own = pl.pallas_call(
        hidden_kernel, name="hidden", out_shape=side, compiler_params=PARAMS
    )(*ring_terms(partials))
    h_pieces = ring_gathered(h_own)
    summed = pl.pallas_call(
        outer_kernel,
        name="outer",
        out_shape=shape((packed_rows, width), BF16),
        compiler_params=PARAMS,
        cost_estimate=cost(3 * product, 2 * stacked * model_width),
    )(*h_pieces, *all_w)
    returned = swapped(summed, experts)

    def weight_grads(name, first, count, pieces):
        return pl.pallas_call(
            functools.partial(weight_kernel, first),
            name=name,
            in_specs=[SMEM] + [VMEM] * 6,
            out_specs=(VMEM,) * count,
            out_shape=(shape(w_gate.shape, BF16),) * count,
            compiler_params=PARAMS,
            cost_estimate=cost(count * product, 2 * model_width * (rows + count * hidden)),
        )(quarter, h_own, *pieces)

    grad_gate, grad_up = weight_grads("weights_in", 0, 2, ring_gathered(after(x_own, h_pieces[3])))
    (grad_down,) = weight_grads("weights_down", 2, 1, ring_gathered(after(g_own, h_pieces[4])))

    packed = pl.pallas_call(
        combine_kernel,
        name="combine",
        grid_spec=pltpu.PrefetchScalarGridSpec(
            num_scalar_prefetch=1,
            grid=(1,),
            in_specs=[
                pl.BlockSpec((count, chosen), whole),
                pl.BlockSpec((count, chosen), whole),
                pl.BlockSpec((count, width), mine),
                pl.BlockSpec((packed_rows, width), whole),
            ],
            out_specs=pl.BlockSpec((2 * count, width + 128), whole),
        ),
        out_shape=shape((2 * count, width + 128), BF16),
        compiler_params=PARAMS,
    )(quarter, expert_ids, gates, grad_out, returned)
    layer_out, gate_grads, token_grads = pl.pallas_call(
        finish_kernel,
        name="finish",
        in_specs=[SMEM] + [VMEM] * 4,
        out_specs=(VMEM,) * 3,
        out_shape=(
            shape((count, model_width), BF16),
            shape((count, chosen), F32),
            shape((count, model_width), BF16),
        ),
        compiler_params=PARAMS,
    )(quarter, packed, moved(packed, 1), moved(packed, 3), moved(packed, 2))
    return layer_out, gate_grads, token_grads, grad_gate, grad_up, grad_down


def solution(mesh):
    rows, cut = P("ep", None), P("ep", "tp", None)
    return jax.shard_map(
        on_device,
        mesh=mesh,
        in_specs=(rows, rows, rows, cut, cut, cut, rows),
        out_specs=(rows, rows, rows, cut, cut, cut),
        check_vma=False,
    )
```

```python
import functools

import jax
import jax.numpy as jnp
from jax import lax
from jax.experimental import pallas as pl
from jax.experimental.pallas import tpu as pltpu
from jax.sharding import PartitionSpec as P

SLOTS = 4
BLOCK = 2 * SLOTS
AHEAD_IN = (0, 3, 1, 2)
AHEAD_OUT = (2, 1, 3, 0)
NN = (((1,), (0,)), ((), ()))
NT = (((1,), (1,)), ((), ()))
TN = (((0,), (0,)), ((), ()))
F32 = jnp.float32
BF16 = jnp.bfloat16
ANY = pl.BlockSpec(memory_space=pl.ANY)
VMEM = pl.BlockSpec(memory_space=pltpu.VMEM)
SMEM = pl.BlockSpec(memory_space=pltpu.SMEM)
PARAMS = pltpu.CompilerParams(vmem_limit_bytes=20 * 1024 * 1024)


def dot(left, right, dims=NN):
    return lax.dot_general(left, right, dims, preferred_element_type=F32)


def cost(flops, moved):
    return pl.CostEstimate(flops=flops, bytes_accessed=moved, transcendentals=0)


def row_facts(shape, dim):
    row = lax.broadcasted_iota(jnp.int32, shape, dim)
    second = lax.rem(lax.div(row, SLOTS), 2) == 1
    return lax.div(row, BLOCK), lax.rem(row, SLOTS).astype(F32), second


def dispatch_kernel(quarter, ids_ref, gates_ref, tok_ref, dy_ref, out_ref):
    chosen, count = ids_ref.shape
    shape = (out_ref.shape[0], count)
    expert, slot, second = row_facts(shape, 0)
    named = jnp.zeros(shape, F32)
    gate = jnp.zeros(shape, F32)
    for k in range(chosen):
        hit = ids_ref[k : k + 1, :] == expert
        named = named + jnp.where(hit, 1.0, 0.0)
        gate = gate + jnp.where(hit, gates_ref[k : k + 1, :], 0.0)
    cols = lax.broadcasted_iota(jnp.int32, (count, count), 1)
    earlier = jnp.where(lax.broadcasted_iota(jnp.int32, (count, count), 0) < cols, 1.0, 0.0)
    before = dot(named.astype(BF16), earlier.astype(BF16))
    pick = jnp.where(before == slot, named, 0.0)
    scale = jnp.sum(pick * jnp.where(second, gate, 1.0), axis=1, keepdims=True)
    pick_x = jnp.where(second, 0.0, pick).astype(BF16)
    pick_g = jnp.where(second, pick, 0.0).astype(BF16)
    rows = dot(pick_x, tok_ref[...]) + dot(pick_g, dy_ref[...])
    out_ref[...] = (scale * rows).astype(BF16)


def placing(packed, rows, kind, packed_dim):
    shape = (packed, rows) if packed_dim == 0 else (rows, packed)
    far = lax.broadcasted_iota(jnp.int32, shape, packed_dim)
    near = lax.broadcasted_iota(jnp.int32, shape, 1 - packed_dim)
    place = lax.div(near, SLOTS) * BLOCK + kind * SLOTS + lax.rem(near, SLOTS)
    return jnp.where(far == place, 1.0, 0.0).astype(BF16)


def unpack_kernel(in_ref, x_ref, g_ref):
    for kind, out_ref in enumerate((x_ref, g_ref)):
        pick = placing(in_ref.shape[0], out_ref.shape[0], kind, 1)
        out_ref[...] = dot(pick, in_ref[...]).astype(BF16)


def columns(q_ref, ahead, width):
    start = lax.rem(q_ref[0] + ahead, 4) * width
    return pl.ds(pl.multiple_of(start, width), width)


def share_kernel(sent, q_ref, wg_ref, wu_ref, wd_ref, *refs):
    outs, sems = refs[:-1], refs[-1]
    hidden = wg_ref.shape[1]
    width = outs[0].shape[1]
    half = hidden // 2
    weights = (wg_ref, wu_ref, wd_ref)
    every, low, high = slice(0, hidden), slice(0, half), slice(half, hidden)

    def upper(ref, first, ahead):
        return [(ref, first, 0, every, ahead), (ref, first + hidden, 1, low, ahead)]

    def lower(ref, first, ahead):
        return [(ref, first, 1, high, ahead), (ref, first + half, 2, every, ahead)]

    middle = hidden + half
    plan = upper(outs[0], 0, 2) + lower(outs[1], 0, 2) if sent else []
    for ref, ahead in zip(outs, (1, 3) if sent else (0,)):
        first = middle if sent else 0
        plan += upper(ref, first, ahead) + lower(ref, first + middle, ahead)
    copies = [
        pltpu.make_async_copy(
            weights[n].at[0, span, columns(q_ref, ahead, width)],
            ref.at[first : first + span.stop - span.start],
            sems.at[m],
        )
        for m, (ref, first, n, span, ahead) in enumerate(plan)
    ]
    for copy in copies:
        copy.start()
    for copy in copies:
        copy.wait()


def weight_parts(own, left, right, top, bottom):
    half = top.shape[0]
    return (
        (top, bottom),
        (right.at[half : 2 * half], right.at[2 * half : 3 * half]),
        (left.at[half : 2 * half], left.at[2 * half : 3 * half]),
        (own.at[0:half], own.at[half : 2 * half]),
    )


def inner_kernel(x_ref, g_ref, *refs):
    weights, (far_t, far_b, right, left, own) = weight_parts(*refs[:5]), refs[5:]
    half = far_t.shape[0]
    cut = half // 3
    outs = [(far_t, far_b)]
    outs += [(ref.at[0:half], ref.at[half : 2 * half]) for ref in (right, left, own)]
    x, g = x_ref[...], g_ref[...]
    for (upper, lower), (upper_out, lower_out) in zip(weights, outs):
        upper_out[...] = dot(upper[...], x, NT).astype(BF16)
        lower_out[0:cut, :] = dot(lower[0:cut, :], x, NT).astype(BF16)
        lower_out[cut:half, :] = dot(lower[cut:half, :], g, NT).astype(BF16)


def hidden_kernel(own_ref, left_ref, right_ref, out_ref):
    total = own_ref[...].astype(F32) + left_ref[...].astype(F32) + right_ref[...].astype(F32)
    hidden = out_ref.shape[0] // 3
    a, b, dh = (total[n * hidden : (n + 1) * hidden] for n in range(3))
    sig = jax.nn.sigmoid(a)
    act = a * sig
    d_gate = dh * b * sig * (1.0 + a * (1.0 - sig))
    for n, value in enumerate((d_gate, dh * act, act * b)):
        out_ref[n * hidden : (n + 1) * hidden, :] = value.astype(BF16)


def outer_kernel(own, left, right, far_t, far_b, *refs):
    weights, out_ref = weight_parts(*refs[:5]), refs[5]
    half = far_t.shape[0]
    cut = half // 3
    sides = [(far_t, far_b)]
    sides += [(ref.at[0:half], ref.at[half : 2 * half]) for ref in (right, left, own)]
    r_rows, y_rows = None, None
    for (upper, lower), (upper_h, lower_h) in zip(weights, sides):
        new = dot(upper_h[...], upper[...], TN) + dot(lower_h[0:cut, :], lower[0:cut, :], TN)
        r_rows = new if r_rows is None else r_rows + new
        new = dot(lower_h[cut:half, :], lower[cut:half, :], TN)
        y_rows = new if y_rows is None else y_rows + new
    total = None
    for kind, value in enumerate((y_rows, r_rows)):
        new = dot(placing(out_ref.shape[0], value.shape[0], kind, 0), value.astype(BF16))
        total = new if total is None else total + new
    out_ref[...] = total.astype(BF16)


def weight_kernel(first, q_ref, h_ref, own, left, right, far_t, far_b, *outs):
    hidden = h_ref.shape[0] // 3
    rows, width = own.shape
    half = rows // 2
    for n, out_ref in enumerate(outs):
        side = h_ref[(first + n) * hidden : (first + n + 1) * hidden, :]
        for piece, ahead in zip((own, left, right), AHEAD_IN):
            out_ref[0, :, columns(q_ref, ahead, width)] = dot(side, piece[...]).astype(BF16)
        far = dot(side[:, :half], far_t[...]) + dot(side[:, half:], far_b[...])
        out_ref[0, :, columns(q_ref, AHEAD_IN[3], width)] = far.astype(BF16)


def combine_kernel(quarter, ids_ref, gates_ref, dy_ref, rows_ref, out_ref):
    count, chosen = ids_ref.shape
    width = dy_ref.shape[1]
    rows = rows_ref[...]
    shape = (count, rows.shape[0])
    expert, slot, second = row_facts(shape, 1)
    hits = [ids_ref[:, k : k + 1] == expert for k in range(chosen)]
    named = jnp.zeros(shape, F32)
    gate = jnp.zeros(shape, F32)
    for k in range(chosen):
        named = named + jnp.where(hits[k], 1.0, 0.0)
        gate = gate + jnp.where(hits[k], gates_ref[:, k : k + 1], 0.0)
    earlier = lax.broadcasted_iota(jnp.int32, (count, count), 1) < lax.broadcasted_iota(
        jnp.int32, (count, count), 0
    )
    before = dot(jnp.where(earlier, 1.0, 0.0).astype(BF16), named.astype(BF16))
    pick = jnp.where(before == slot, named, 0.0)
    pick_y = jnp.where(second, 0.0, pick)
    pick_r = jnp.where(second, pick, 0.0).astype(BF16)
    weight = pick_y * gate
    high = weight.astype(BF16)
    low = (weight - high.astype(F32)).astype(BF16)
    out_ref[0:count, 0:width] = (dot(high, rows) + dot(low, rows)).astype(BF16)
    out_ref[count : 2 * count, 0:width] = dot(pick_r, rows).astype(BF16)
    products = pick_y * dot(dy_ref[...], rows, NT)
    lane = lax.broadcasted_iota(jnp.int32, (count, 128), 1)
    share = jnp.zeros((count, 128), F32)
    for k in range(chosen):
        value = jnp.sum(jnp.where(hits[k], products, 0.0), axis=1, keepdims=True)
        share = share + jnp.where(lax.rem(lane, chosen) == k, value, 0.0)
    first = share.astype(BF16).astype(F32)
    rest = share - first
    middle = rest.astype(BF16).astype(F32)
    parts = jnp.where(lane < chosen, first, jnp.where(lane < 2 * chosen, middle, rest - middle))
    out_ref[0:count, width : width + 128] = parts.astype(BF16)
    out_ref[count : 2 * count, width : width + 128] = jnp.zeros((count, 128), BF16)


def finish_kernel(q_ref, *refs):
    pieces, (layer_ref, gate_ref, token_ref) = refs[:4], refs[4:]
    count, chosen = gate_ref.shape
    width = layer_ref.shape[1] // 4
    share = jnp.zeros((count, 128), F32)
    for j, ahead in enumerate(AHEAD_IN):
        span = columns(q_ref, ahead, width)
        layer_ref[:, span] = pieces[j][0:count, 0:width]
        token_ref[:, span] = pieces[j][count : 2 * count, 0:width]
        share = share + pieces[j][0:count, width : width + 128].astype(F32)
    total = share[:, 0:chosen]
    for j in range(1, 3):
        total = total + share[:, j * chosen : (j + 1) * chosen]
    gate_ref[...] = total


def moved(value, ahead):
    return lax.ppermute(value, "tp", [(i, (i + ahead) % 4) for i in range(4)])


def ring_gathered(own):
    half = own.shape[0] // 2
    left, right = moved(own, 1), moved(own, 3)
    far_t, far_b = moved(left[:half], 1), moved(right[half:], 3)
    return own, left, right, far_t, far_b


def added(a, b):
    return (a.astype(F32) + b.astype(F32)).astype(BF16)


def after(value, other):
    return lax.optimization_barrier((value, other))[0]


def ring_terms(partials):
    far_t, far_b, right, left, own = partials
    half = far_t.shape[0]
    in_t, in_b = moved(far_t, 1), moved(far_b, 3)
    from_left = moved(jnp.concatenate([added(right[:half], in_t), right[half:]]), 1)
    from_right = moved(jnp.concatenate([left[:half], added(left[half:], in_b)]), 3)
    return own, from_left, from_right


def swapped(rows, experts):
    block = rows.reshape(experts, BLOCK, rows.shape[-1])
    return lax.all_to_all(block, "ep", 0, 0, tiled=True).reshape(rows.shape)


def on_device(tokens, expert_ids, gates, w_gate, w_up, w_down, grad_out):
    count, model_width = tokens.shape
    chosen = expert_ids.shape[1]
    hidden = w_gate.shape[1]
    experts = lax.axis_size("ep")
    width = model_width // 4
    packed_rows, rows = experts * BLOCK, experts * SLOTS
    quarter = lax.axis_index("tp").astype(jnp.int32).reshape(1)
    shape = jax.ShapeDtypeStruct

    stacked = 3 * hidden
    sends = shape((stacked * 3 // 2, width), BF16)

    def shares(name, sent, *shapes):
        return pl.pallas_call(
            functools.partial(share_kernel, sent),
            name=name,
            in_specs=[SMEM] + [ANY] * 3,
            out_specs=(VMEM,) * len(shapes),
            scratch_shapes=[pltpu.SemaphoreType.DMA((12,))],
            out_shape=shapes,
            compiler_params=pltpu.CompilerParams(vmem_limit_bytes=(60 if sent else 20) * 1024 * 1024),
        )

    to_right, to_left = shares("share", True, sends, sends)(quarter, w_gate, w_up, w_down)
    (own_w,) = shares("share_own", False, shape((stacked, width), BF16))(
        quarter, w_gate, w_up, after(w_down, to_right)
    )
    left_w, right_w = moved(to_right, 1), moved(to_left, 3)
    far_w = moved(left_w[: stacked // 2], 1), moved(right_w[: stacked // 2], 3)
    all_w = (own_w, left_w, right_w) + far_w
    tokens = after(tokens, to_right)

    whole = lambda i, q: (0, 0)
    mine = lambda i, q: (0, q[0])
    sent = pl.pallas_call(
        dispatch_kernel,
        name="dispatch",
        grid_spec=pltpu.PrefetchScalarGridSpec(
            num_scalar_prefetch=1,
            grid=(1,),
            in_specs=[
                pl.BlockSpec((chosen, count), whole),
                pl.BlockSpec((chosen, count), whole),
                pl.BlockSpec((count, width), mine),
                pl.BlockSpec((count, width), mine),
            ],
            out_specs=pl.BlockSpec((packed_rows, width), whole),
        ),
        out_shape=shape((packed_rows, width), BF16),
        compiler_params=pltpu.CompilerParams(vmem_limit_bytes=60 * 1024 * 1024),
    )(quarter, expert_ids.T, gates.T, tokens, grad_out)
    piece = shape((rows, width), BF16)
    x_own, g_own = pl.pallas_call(
        unpack_kernel, name="unpack", out_shape=(piece, piece), compiler_params=PARAMS
    )(swapped(sent, experts))

    product = 2 * rows * hidden * model_width
    side, part = shape((stacked, rows), BF16), shape((stacked // 2, rows), BF16)
    partials = pl.pallas_call(
        inner_kernel,
        name="inner",
        out_shape=(part, part, side, side, side),
        compiler_params=PARAMS,
        cost_estimate=cost(3 * product, 2 * stacked * model_width),
    )(x_own, g_own, *all_w)
    h_own = pl.pallas_call(
        hidden_kernel, name="hidden", out_shape=side, compiler_params=PARAMS
    )(*ring_terms(partials))
    h_pieces = ring_gathered(h_own)
    summed = pl.pallas_call(
        outer_kernel,
        name="outer",
        out_shape=shape((packed_rows, width), BF16),
        compiler_params=PARAMS,
        cost_estimate=cost(3 * product, 2 * stacked * model_width),
    )(*h_pieces, *all_w)
    returned = swapped(summed, experts)

    def weight_grads(name, first, count, pieces):
        return pl.pallas_call(
            functools.partial(weight_kernel, first),
            name=name,
            in_specs=[SMEM] + [VMEM] * 6,
            out_specs=(VMEM,) * count,
            out_shape=(shape(w_gate.shape, BF16),) * count,
            compiler_params=PARAMS,
            cost_estimate=cost(count * product, 2 * model_width * (rows + count * hidden)),
        )(quarter, h_own, *pieces)

    x_pieces = ring_gathered(after(x_own, h_pieces[3]))
    grad_gate, grad_up = weight_grads("weights_in", 0, 2, x_pieces)
    (grad_down,) = weight_grads("weights_down", 2, 1, ring_gathered(after(g_own, x_pieces[1])))

    packed = pl.pallas_call(
        combine_kernel,
        name="combine",
        grid_spec=pltpu.PrefetchScalarGridSpec(
            num_scalar_prefetch=1,
            grid=(1,),
            in_specs=[
                pl.BlockSpec((count, chosen), whole),
                pl.BlockSpec((count, chosen), whole),
                pl.BlockSpec((count, width), mine),
                pl.BlockSpec((packed_rows, width), whole),
            ],
            out_specs=pl.BlockSpec((2 * count, width + 128), whole),
        ),
        out_shape=shape((2 * count, width + 128), BF16),
        compiler_params=PARAMS,
    )(quarter, expert_ids, gates, grad_out, returned)
    layer_out, gate_grads, token_grads = pl.pallas_call(
        finish_kernel,
        name="finish",
        in_specs=[SMEM] + [VMEM] * 4,
        out_specs=(VMEM,) * 3,
        out_shape=(
            shape((count, model_width), BF16),
            shape((count, chosen), F32),
            shape((count, model_width), BF16),
        ),
        compiler_params=PARAMS,
    )(quarter, packed, moved(packed, 1), moved(packed, 3), moved(packed, 2))
    return layer_out, gate_grads, token_grads, grad_gate, grad_up, grad_down


def solution(mesh):
    rows, cut = P("ep", None), P("ep", "tp", None)
    return jax.shard_map(
        on_device,
        mesh=mesh,
        in_specs=(rows, rows, rows, cut, cut, cut, rows),
        out_specs=(rows, rows, rows, cut, cut, cut),
        check_vma=False,
    )
```
